512 devices in a mesh: seq: 64 (over y, z), head: 8 (over x, core).
Axes of the slice: x: 4, y: 4, z: 16, core: 2. Of those that a mesh axis runs over, the one named last changes fastest.
Arguments:
- queries: bfloat16 [16384, 8192], P(('seq', 'head')), may hold values from -6 to 6
- keys: bfloat16 [16384, 8192], P(('seq', 'head')), may hold values from -6 to 6
- values: bfloat16 [16384, 8192], P(('seq', 'head')), may hold values from -70 to 70
- log_decay: float32 [64, 16384], P('head', 'seq'), may hold values from -1 to 0
- doc_lengths: int32 [32], replicated, may hold values from 1 to 4096, 16384 in all
- gain: float32 [8192], P('head'), may hold values from 0.25 to 1.75
Outputs:
- attended: bfloat16 [16384, 8192], P(('seq', 'head'))
The draws below stay inside these ranges and needn't reach their ends.
All inputs are finite; a program needn't handle non-finite values.
Results may differ from the reference program's by a relative error of at most 0.001.
Values may be sent and summed in bfloat16 or wider, within the bound.
No kernel may reach another device: no remote copies, remote signals or barrier semaphores. Data moves between devices by JAX's collectives and lax.ppermute only.
A program may use at most 128 MiB of HBM per device.

```python
import functools
import math
import jax
import jax.numpy as jnp
import numpy as np
from jax import lax

HEAD_TOTAL = 64
DH = 128
TOK_DEV = 256
NDOC = 32
TOKEN_TOTAL = 16384


def draw_values(key, part):
    key_base, key_cols = jax.random.split(key, 2)
    column_scale = jnp.exp(jax.random.uniform(key_cols, (HEAD_TOTAL * DH,), jnp.float32, 0.0, math.log(10.0)))
    base = jnp.clip(jax.random.normal(key_base, (TOKEN_TOTAL, HEAD_TOTAL * DH), jnp.float32), -6.0, 6.0)
    return (base * column_scale[None, :]).astype(jnp.bfloat16)


def draw_log_decay(key, part):
    every_key = jax.random.split(key, 7)
    fast_share = 0.5
    fast = jax.random.uniform(every_key[0], (HEAD_TOTAL,), jnp.float32) < fast_share
    fast_rate = 1.0 / jax.random.uniform(every_key[1], (HEAD_TOTAL,), jnp.float32, 30.0, 50.0)
    slow_rate = jnp.exp(jax.random.uniform(every_key[2], (HEAD_TOTAL,), jnp.float32, math.log(0.05), math.log(0.2))) / TOKEN_TOTAL
    decay_rate = jnp.where(fast, fast_rate, slow_rate)
    per_token_decay = jnp.exp(jax.random.uniform(every_key[3], (HEAD_TOTAL, TOKEN_TOTAL), jnp.float32, -0.7, 0.7))
    segment_decay_factor = jnp.exp(jax.random.uniform(every_key[4], (HEAD_TOTAL, TOKEN_TOTAL // TOK_DEV), jnp.float32, -0.7, 0.7))
    segment_decay_factor = jnp.repeat(segment_decay_factor, TOK_DEV, axis=1)
    segment_offsets = jax.random.randint(every_key[5], (3,), 0, TOKEN_TOTAL)
    segment_length = jnp.log(jax.random.uniform(every_key[6], (3, HEAD_TOTAL), jnp.float32, 0.6, 0.8))
    token_positions = jnp.arange(TOKEN_TOTAL, dtype=jnp.int32)
    boundary_hits = (token_positions[None, :] == segment_offsets[:, None]).astype(jnp.float32)
    segment_count = jnp.sum(segment_length[:, :, None] * boundary_hits[:, None, :], axis=0)
    return -decay_rate[:, None] * per_token_decay * segment_decay_factor + segment_count


def levels(own_key, dims, cuts, low, top_value):
    def one(position, parts):
        steps = jax.random.uniform(jax.random.fold_in(jax.random.fold_in(own_key, 6), position), (parts,), jnp.float32, low / len(cuts), top_value / len(cuts))
        return jnp.repeat(jnp.exp(steps), dims[position] // parts).reshape((-1,) + (1,) * (len(dims) - position - 1))

    factor_of = one(*cuts[0])
    for cut in cuts[1:]:
        factor_of = factor_of * one(*cut)
    return factor_of


def split_up(amount, total, bound, lean):
    weights = [(1 << 20) // math.isqrt(standing ** lean) + 1 for standing in range(2, amount + 1)]
    rest, holding = total - bound - (amount - 1), [1] * (amount - 1)
    while rest > 0:
        candidates = [i for i in range(amount - 1) if holding[i] < bound]
        whole, left = sum([weights[i] for i in candidates]), rest
        for i in candidates:
            addition = min(bound - holding[i], max(1, left * weights[i] // whole), rest)
            holding[i] = holding[i] + addition
            rest = rest - addition
    return np.array([bound] + holding)


def ragged(stream_key, count, total, most, lean):
    if count == 2:
        one = jax.random.randint(stream_key, (), max(1, total - most), min(most, total - 1) + 1)
        return jnp.stack([one, total - one])
    lengths = jnp.asarray(split_up(count, total, most, lean), jnp.int32)
    couples = (count - 1) // 2
    source_of, receiver = lengths[1:1 + 2 * couples:2], lengths[2:2 + 2 * couples:2]
    margin = jnp.minimum(source_of - 1, most - receiver)
    passed = jax.random.randint(jax.random.fold_in(stream_key, 1), (couples,), 0, 1 << 20) % (margin + 1)
    lengths = lengths.at[1:1 + 2 * couples:2].set(source_of - passed).at[2:2 + 2 * couples:2].set(receiver + passed)
    return lengths[jax.random.permutation(jax.random.fold_in(stream_key, 2), count)]


def scatter_about(key, dims, scale, reach, cuts=(), held_as=jnp.bfloat16):
    values = scale * jax.random.normal(key, dims, jnp.float32)
    if cuts:
        values = values * levels(key, dims, cuts, -0.22, 0.18)
    return jnp.clip(values, -reach, reach).astype(held_as)


def setup_inputs(seed: int = 0) -> dict:
    seeds = jax.random.split(jax.random.key(seed), 7)
    return {
        "queries": scatter_about(seeds[0], (TOKEN_TOTAL, HEAD_TOTAL * DH), 1.0, 6.0, ((0, 512),)),
        "keys": scatter_about(seeds[1], (TOKEN_TOTAL, HEAD_TOTAL * DH), 1.0, 6.0, ((0, 512),)),
        "values": draw_values(jax.random.fold_in(seeds[6], 71), 0),
        "log_decay": draw_log_decay(jax.random.fold_in(seeds[6], 71), 0),
        "doc_lengths": ragged(seeds[4], NDOC, TOKEN_TOTAL, TOKEN_TOTAL // 4, 2).astype(jnp.int32),
        "gain": jnp.clip(1.0 + 0.15 * jax.random.normal(seeds[5], (HEAD_TOTAL * DH,), jnp.float32), 0.25, 1.75),
    }


HIGHEST = lax.Precision.HIGHEST

def block_step(gain_table, state, pieces):
    query_rows, key_rows, value_rows, decays, doc_block, previous = pieces
    query_rows = query_rows.astype(jnp.float32)
    key_rows = key_rows.astype(jnp.float32)
    value_rows = value_rows.astype(jnp.float32)
    decay_sum = jnp.cumsum(decays, axis=0)
    block_size = doc_block.shape[0]
    order_ids = jnp.arange(block_size, dtype=jnp.int32)
    allowed = (order_ids[:, None] >= order_ids[None, :]) & (doc_block[:, None] == doc_block[None, :])
    spread_mask = allowed[:, :, None]
    gaps = decay_sum[:, None, :] - decay_sum[None, :, :]
    weights = jnp.where(spread_mask, jnp.exp(jnp.where(spread_mask, gaps, 0.0)), 0.0)
    scores = jnp.einsum('ihd,jhd->ijh', query_rows, key_rows, precision=HIGHEST) * weights
    within = jnp.einsum('ijh,jhd->ihd', scores, value_rows, precision=HIGHEST)
    joined = (doc_block == previous).astype(decays.dtype)
    leading = jnp.exp(decay_sum) * joined[:, None]
    across = jnp.einsum('ihd,hde->ihe', query_rows * leading[:, :, None], state, precision=HIGHEST)
    tailing = jnp.exp(decay_sum[-1][None, :] - decay_sum) * (doc_block == doc_block[-1]).astype(decays.dtype)[:, None]
    local_state = jnp.einsum('jhd,jhe->hde', key_rows * tailing[:, :, None], value_rows, precision=HIGHEST)
    carried = jnp.exp(decay_sum[-1]) * (doc_block[-1] == previous).astype(decays.dtype)
    mixed = within + across
    mean_square = lax.optimization_barrier(jnp.mean(mixed * mixed, axis=-1, keepdims=True))
    normed = mixed * lax.rsqrt(mean_square + 1e-06) * gain_table[None, :, :]
    return (carried[:, None, None] * state + local_state, normed.astype(jnp.bfloat16))

def reference(queries, keys, values, log_decay, doc_lengths, gain):
    step_size = math.gcd(TOKEN_TOTAL, 128)
    blocks = TOKEN_TOTAL // step_size
    doc_ends = jnp.cumsum(doc_lengths).astype(jnp.int32)
    positions = jnp.arange(TOKEN_TOTAL, dtype=jnp.int32)
    doc_ids = lax.optimization_barrier(jnp.sum((doc_ends[None, :] <= positions[:, None]).astype(jnp.int32), axis=1)).astype(jnp.int32)
    doc_grid = doc_ids.reshape(blocks, step_size)
    previous = jnp.concatenate([jnp.full((1,), -1, jnp.int32), doc_grid[:-1, -1].astype(jnp.int32)])
    query_grid = queries.reshape(blocks, step_size, HEAD_TOTAL, DH)
    key_grid = keys.reshape(blocks, step_size, HEAD_TOTAL, DH)
    value_grid = values.reshape(blocks, step_size, HEAD_TOTAL, DH)
    decay_grid = log_decay.T.reshape(blocks, step_size, HEAD_TOTAL)
    initial = jnp.zeros((HEAD_TOTAL, DH, DH), jnp.float32)
    gain_table = gain.reshape(HEAD_TOTAL, DH)
    stepper = functools.partial(block_step, gain_table)
    final_state, outputs = lax.scan(stepper, initial, (query_grid, key_grid, value_grid, decay_grid, doc_grid, previous))
    return outputs.reshape(TOKEN_TOTAL, HEAD_TOTAL * DH)
```

```python
import functools

import jax
import jax.numpy as jnp
from jax import lax
from jax.experimental import pallas as pl
from jax.experimental.pallas import tpu as pltpu
from jax.sharding import PartitionSpec as P

F32 = jnp.float32
BF16 = jnp.bfloat16
DH = 128
CH = 128
NC = 4
PAIR = 2
NH = 4
SEG = CH * NC
GROUP = 16
ROWS = 16
VMEM_LIMIT = 48 * 1024 * 1024


def split2(x):
    high = x.astype(BF16)
    return high, (x - high.astype(F32)).astype(BF16)


def split3(x):
    high = x.astype(BF16)
    rest = x - high.astype(F32)
    mid = rest.astype(BF16)
    return high, mid, (rest - mid.astype(F32)).astype(BF16)


def dot(a, b):
    return jnp.dot(a, b, preferred_element_type=F32)


def pack_kernel(q_ref, k_ref, v_ref, out_ref, sems):
    copies = []
    for place in range(GROUP):
        column = (2 * (place % 8) + place // 8) * NH * DH
        for which, ref in enumerate((q_ref, k_ref, v_ref)):
            copies.append(
                pltpu.make_async_copy(
                    ref.at[:, pl.ds(column, NH * DH)],
                    out_ref.at[place, which],
                    sems.at[place, which],
                )
            )
    for copy in copies:
        copy.start()
    for copy in copies:
        copy.wait()


def unpack_kernel(in_ref, out_ref, sems):
    copies = []
    for place in range(GROUP):
        column = (2 * (place % 8) + place // 8) * NH * DH
        copies.append(
            pltpu.make_async_copy(
                in_ref.at[place], out_ref.at[:, pl.ds(column, NH * DH)], sems.at[place]
            )
        )
    for copy in copies:
        copy.start()
    for copy in copies:
        copy.wait()


def pick_heads(tile, half):
    return jnp.where(half == 0, tile, pltpu.roll(tile, 4, axis=0))


def state_kernel(place_ref, lengths_ref, own_ref, other_ref, k_ref, v_ref, send_ref, rows_ref, cols_ref):
    segment, half = place_ref[0], place_ref[1]
    own, other = own_ref[...], other_ref[...]
    first = jnp.where(half == 0, own, other)
    second = jnp.where(half == 0, other, own)
    decay = jnp.concatenate(
        [
            pick_heads(part[:, i * CH : (i + 1) * CH], half)
            for part in (first, second)
            for i in range(2)
        ],
        axis=0,
    )
    upper = (
        lax.broadcasted_iota(jnp.int32, (CH, CH), 0) <= lax.broadcasted_iota(jnp.int32, (CH, CH), 1)
    ).astype(BF16)
    high, mid, low = split3(decay)
    sums = dot(high, upper) + (dot(mid, upper) + dot(low, upper))

    lane = lax.broadcasted_iota(jnp.int32, (8, CH), 1)
    start = segment * SEG
    spots = [jnp.full((8, CH), start - 1, jnp.int32)] + [start + c * CH + lane for c in range(NC)]
    ids = [jnp.zeros((8, CH), jnp.int32) for _ in spots]
    end = jnp.int32(0)
    for d in range(lengths_ref.shape[0]):
        end = end + lengths_ref[d]
        ids = [i + (end <= s).astype(jnp.int32) for i, s in zip(ids, spots)]

    def last(tile):
        return jnp.broadcast_to(tile[:, CH - 1 : CH], (8, CH))

    prior = ids[0]
    tails, leads, carries = [], [], []
    for c in range(NC):
        local, here = sums[8 * c : 8 * c + 8], ids[c + 1]
        total, closing = last(local), last(here)
        tails.append(jnp.where(here == closing, jnp.exp(total - local), 0.0))
        leads.append(jnp.where(here == prior, jnp.exp(local), 0.0))
        carries.append(jnp.where(closing == prior, jnp.exp(total), 0.0))
        prior = closing
    before = [jnp.ones((8, CH), F32)]
    for c in range(NC):
        before.append(before[-1] * carries[c])
    after = [jnp.ones((8, CH), F32)]
    for c in range(NC - 1, 0, -1):
        after.append(after[-1] * carries[c])
    after = after[::-1]
    rows_ref[0:32] = sums
    rows_ref[32:64] = jnp.concatenate(tails, axis=0)
    rows_ref[64:96] = jnp.concatenate(carries, axis=0)
    rows_ref[96:128] = jnp.concatenate([i.astype(F32) for i in ids[1:]], axis=0)
    table = jnp.concatenate(
        [sums]
        + leads
        + [lead * b for lead, b in zip(leads, before)]
        + [i.astype(F32) for i in ids[1:]],
        axis=0,
    )
    cols_ref[...] = table.T

    full_tails = [t * a for t, a in zip(tails, after)]
    for head in range(NH):
        at = slice(head * DH, (head + 1) * DH)
        key_part = k_ref[:, 0, :, at].reshape(SEG, DH)
        value_part = v_ref[:, 0, :, at].reshape(SEG, DH)
        weight = jnp.concatenate([t[head : head + 1] for t in full_tails], axis=1)
        weighted = key_part.T.astype(F32) * weight
        both = dot(jnp.concatenate(split2(weighted), axis=0), value_part)
        state = both[:DH] + both[DH:]
        factor = jnp.broadcast_to(before[NC][head : head + 1], (8, DH))
        for piece in range(DH // ROWS):
            send_ref[head * (DH // ROWS) + piece, :ROWS] = state[piece * ROWS : (piece + 1) * ROWS]
            send_ref[head * (DH // ROWS) + piece, ROWS:] = factor


def near_kernel(q_ref, k_ref, v_ref, rows_ref, cols_ref, near_ref):
    order = lax.broadcasted_iota(jnp.int32, (CH, CH), 0) >= lax.broadcasted_iota(
        jnp.int32, (CH, CH), 1
    )
    cols = cols_ref[...]
    masks = []
    for c in range(NC):
        ids_row = rows_ref[96 + 8 * c : 97 + 8 * c]
        ids_col = cols[:, 96 + 8 * c : 97 + 8 * c]
        masks.append(order & (ids_col == ids_row))
    for head in range(NH):
        at = slice(head * DH, (head + 1) * DH)
        state = None
        for c in range(NC):
            part = slice(4 * c, 4 * c + 4)
            row = 8 * c + head
            query = q_ref[part, 0, :, at].reshape(CH, DH)
            key_part = k_ref[part, 0, :, at].reshape(CH, DH)
            value_part = v_ref[part, 0, :, at].reshape(CH, DH)
            keys_across = key_part.T
            gaps = cols[:, row : row + 1] - rows_ref[row : row + 1]
            weights = jnp.where(masks[c], jnp.exp(jnp.where(masks[c], gaps, 0.0)), 0.0)
            high, low = split2(dot(query, keys_across) * weights)
            mixed = dot(high, value_part) + dot(low, value_part)
            if c:
                both = dot(query, jnp.concatenate(split2(state), axis=1))
                mixed = mixed + (both[:, :DH] + both[:, DH:]) * cols[:, 32 + row : 33 + row]
            near_ref[head, c * CH : (c + 1) * CH] = mixed
            if c < NC - 1:
                weighted = keys_across.astype(F32) * rows_ref[32 + row : 33 + row]
                both = dot(jnp.concatenate(split2(weighted), axis=0), value_part)
                own = both[:DH] + both[DH:]
                state = own if c == 0 else own + state * rows_ref[64 + row : 65 + row]


def scan_kernel(in_ref, out_ref):
    state = jnp.zeros((ROWS, DH), F32)
    for segment in range(in_ref.shape[0]):
        out_ref[segment] = state
        factor = in_ref[segment, ROWS : ROWS + 1]
        state = state * factor + in_ref[segment, :ROWS]


def close_kernel(place_ref, q_ref, state_ref, near_ref, cols_ref, gain_ref, out_ref):
    gain = pick_heads(gain_ref[...], place_ref[1])
    cols = cols_ref[...]
    for head in range(NH):
        at = slice(head * DH, (head + 1) * DH)
        query = q_ref[:, 0, :, at].reshape(SEG, DH)
        both = dot(query, jnp.concatenate(split2(state_ref[head]), axis=1))
        far = both[:, :DH] + both[:, DH:]
        for c in range(NC):
            column = 64 + 8 * c + head
            mixed = near_ref[head, c * CH : (c + 1) * CH] + far[c * CH : (c + 1) * CH] * (
                cols[:, column : column + 1]
            )
            square = jnp.mean(mixed * mixed, axis=-1, keepdims=True)
            normed = mixed * lax.rsqrt(square + 1e-06) * gain[head : head + 1]
            out_ref[4 * c : 4 * c + 4, :, at] = normed.astype(BF16).reshape(4, CH // 4, DH)


VMEM = pl.BlockSpec(memory_space=pltpu.VMEM)
SMEM = pl.BlockSpec(memory_space=pltpu.SMEM)
ANY = pl.BlockSpec(memory_space=pl.ANY)
PARAMS = pltpu.CompilerParams(vmem_limit_bytes=VMEM_LIMIT)


def part_spec(which):
    return pl.BlockSpec((GROUP, 1, SEG // GROUP, NH * DH), lambda i: (0, which, 0, 0))


def whole(*shape):
    return pl.BlockSpec(shape, lambda i: (0,) * len(shape))


def shaped(shape, kind=F32):
    return jax.ShapeDtypeStruct(shape, kind)


def local(seq_size, head_size, queries, keys, values, log_decay, doc_lengths, gain):
    tokens = queries.shape[0]
    segments = seq_size // PAIR
    pieces = NH * DH // ROWS
    seq = lax.axis_index("seq")
    place = jnp.stack([seq // PAIR, seq % PAIR]).astype(jnp.int32)
    token_groups = [
        [g * GROUP + i for i in range(GROUP)] for g in range(seq_size * head_size // GROUP)
    ]
    scan_groups = [[g * PAIR + i for g in range(segments)] for i in range(PAIR)]

    other_decay = lax.ppermute(log_decay, "seq", [(s, s ^ 1) for s in range(seq_size)])
    sent = pl.pallas_call(
        pack_kernel,
        out_shape=shaped((GROUP, 3, tokens, NH * DH), BF16),
        in_specs=[ANY] * 3,
        out_specs=ANY,
        scratch_shapes=[pltpu.SemaphoreType.DMA((GROUP, 3))],
        name="pack",
    )(queries, keys, values)
    parts = lax.all_to_all(
        sent, ("seq", "head"), 0, 0, axis_index_groups=token_groups, tiled=True
    )
    own, rows, cols = pl.pallas_call(
        state_kernel,
        out_shape=(
            shaped((pieces, ROWS + 8, DH)),
            shaped((128, CH)),
            shaped((CH, 128)),
        ),
        grid=(1,),
        in_specs=[SMEM, SMEM, whole(8, SEG // PAIR), whole(8, SEG // PAIR), part_spec(1), part_spec(2)],
        out_specs=(whole(pieces, ROWS + 8, DH), whole(128, CH), whole(CH, 128)),
        compiler_params=PARAMS,
        name="state",
    )(place, doc_lengths, log_decay, other_decay, parts, parts)
    gathered = lax.all_to_all(own, "seq", 0, 0, axis_index_groups=scan_groups, tiled=True)
    near = pl.pallas_call(
        near_kernel,
        out_shape=shaped((NH, SEG, DH)),
        grid=(1,),
        in_specs=[part_spec(0), part_spec(1), part_spec(2), whole(128, CH), whole(CH, 128)],
        out_specs=whole(NH, SEG, DH),
        compiler_params=PARAMS,
        cost_estimate=pl.CostEstimate(flops=500000000, transcendentals=300000, bytes_accessed=4000000),
        name="near",
    )(parts, parts, parts, rows, cols)
    prefixes = pl.pallas_call(
        scan_kernel,
        out_shape=shaped((segments, ROWS, DH)),
        name="scan",
    )(gathered)
    incoming = lax.all_to_all(
        prefixes, "seq", 0, 0, axis_index_groups=scan_groups, tiled=True
    ).reshape(NH, DH, DH)
    normed = pl.pallas_call(
        close_kernel,
        out_shape=shaped((GROUP, tokens, NH * DH), BF16),
        grid=(1,),
        in_specs=[
            SMEM,
            part_spec(0),
            whole(NH, DH, DH),
            whole(NH, SEG, DH),
            whole(CH, 128),
            whole(8, DH),
        ],
        out_specs=whole(GROUP, tokens, NH * DH),
        compiler_params=PARAMS,
        name="close",
    )(place, parts, incoming, near, cols, gain.reshape(8, DH))
    returned = lax.all_to_all(
        normed, ("seq", "head"), 0, 0, axis_index_groups=token_groups, tiled=True
    )
    return pl.pallas_call(
        unpack_kernel,
        out_shape=shaped((tokens, GROUP * NH * DH), BF16),
        in_specs=[ANY],
        out_specs=ANY,
        scratch_shapes=[pltpu.SemaphoreType.DMA((GROUP,))],
        name="unpack",
    )(returned)


def solution(mesh):
    return jax.shard_map(
        functools.partial(local, mesh.shape["seq"], mesh.shape["head"]),
        mesh=mesh,
        in_specs=(
            P(("seq", "head"), None),
            P(("seq", "head"), None),
            P(("seq", "head"), None),
            P("head", "seq"),
            P(),
            P("head"),
        ),
        out_specs=P(("seq", "head"), None),
        check_vma=False,
    )
```

```python
import functools

import jax
import jax.numpy as jnp
from jax import lax
from jax.experimental import pallas as pl
from jax.experimental.pallas import tpu as pltpu
from jax.sharding import PartitionSpec as P

F32 = jnp.float32
BF16 = jnp.bfloat16
DH = 128
CH = 128
NC = 4
PAIR = 2
NH = 4
SEG = CH * NC
GROUP = 16
ROWS = 16
PIECE = ROWS + 1
VMEM_LIMIT = 48 * 1024 * 1024


def split2(x):
    high = x.astype(BF16)
    return high, (x - high.astype(F32)).astype(BF16)


def split3(x):
    high = x.astype(BF16)
    rest = x - high.astype(F32)
    mid = rest.astype(BF16)
    return high, mid, (rest - mid.astype(F32)).astype(BF16)


def dot(a, b):
    return jnp.dot(a, b, preferred_element_type=F32)


def pack_kernel(q_ref, k_ref, v_ref, out_ref):
    for which, ref in enumerate((q_ref, k_ref, v_ref)):
        for part in range(4):
            out_ref[part % 2, part // 2, which] = ref[:, part * NH * DH : (part + 1) * NH * DH]


def unpack_kernel(in_ref, out_ref):
    for part in range(4):
        out_ref[:, part * NH * DH : (part + 1) * NH * DH] = in_ref[part % 2, part // 2]


def pick_heads(tile, half):
    return jnp.where(half == 0, tile, pltpu.roll(tile, 4, axis=0))


def state_kernel(place_ref, lengths_ref, own_ref, other_ref, k_ref, v_ref, send_ref, rows_ref, cols_ref):
    segment, half = place_ref[0], place_ref[1]
    own, other = own_ref[...], other_ref[...]
    first = jnp.where(half == 0, own, other)
    second = jnp.where(half == 0, other, own)
    decay = jnp.concatenate(
        [
            pick_heads(part[:, i * CH : (i + 1) * CH], half)
            for part in (first, second)
            for i in range(2)
        ],
        axis=0,
    )
    upper = (
        lax.broadcasted_iota(jnp.int32, (CH, CH), 0) <= lax.broadcasted_iota(jnp.int32, (CH, CH), 1)
    ).astype(BF16)
    high, mid, low = split3(decay)
    sums = dot(high, upper) + (dot(mid, upper) + dot(low, upper))

    lane = lax.broadcasted_iota(jnp.int32, (8, CH), 1)
    start = segment * SEG
    spots = [jnp.full((8, CH), start - 1, jnp.int32)] + [start + c * CH + lane for c in range(NC)]
    ids = [jnp.zeros((8, CH), jnp.int32) for _ in spots]
    end = jnp.int32(0)
    for d in range(lengths_ref.shape[0]):
        end = end + lengths_ref[d]
        ids = [i + (end <= s).astype(jnp.int32) for i, s in zip(ids, spots)]

    def last(tile):
        return jnp.broadcast_to(tile[:, CH - 1 : CH], (8, CH))

    prior = ids[0]
    tails, leads, carries = [], [], []
    for c in range(NC):
        local, here = sums[8 * c : 8 * c + 8], ids[c + 1]
        total, closing = last(local), last(here)
        tails.append(jnp.where(here == closing, jnp.exp(total - local), 0.0))
        leads.append(jnp.where(here == prior, jnp.exp(local), 0.0))
        carries.append(jnp.where(closing == prior, jnp.exp(total), 0.0))
        prior = closing
    before = [jnp.ones((8, CH), F32)]
    for c in range(NC):
        before.append(before[-1] * carries[c])
    after = [jnp.ones((8, CH), F32)]
    for c in range(NC - 1, 0, -1):
        after.append(after[-1] * carries[c])
    after = after[::-1]
    rows_ref[0:32] = sums
    rows_ref[32:64] = jnp.concatenate(tails, axis=0)
    rows_ref[64:96] = jnp.concatenate(carries, axis=0)
    rows_ref[96:128] = jnp.concatenate([i.astype(F32) for i in ids[1:]], axis=0)
    table = jnp.concatenate(
        [sums]
        + leads
        + [lead * b for lead, b in zip(leads, before)]
        + [i.astype(F32) for i in ids[1:]],
        axis=0,
    )
    cols_ref[...] = table.T

    full_tails = [t * a for t, a in zip(tails, after)]
    for head in range(NH):
        at = slice(head * DH, (head + 1) * DH)
        key_part = k_ref[:, 0, :, at].reshape(SEG, DH)
        value_part = v_ref[:, 0, :, at].reshape(SEG, DH)
        weight = jnp.concatenate([t[head : head + 1] for t in full_tails], axis=1)
        weighted = key_part.T.astype(F32) * weight
        both = dot(jnp.concatenate(split2(weighted), axis=0), value_part)
        state = both[:DH] + both[DH:]
        for piece in range(DH // ROWS):
            place = head * (DH // ROWS) + piece
            for row in range(ROWS):
                send_ref[place, :, row * DH : (row + 1) * DH] = state[
                    piece * ROWS + row : piece * ROWS + row + 1
                ]
            send_ref[place, :, ROWS * DH :] = before[NC][head : head + 1]


def near_kernel(q_ref, k_ref, v_ref, rows_ref, cols_ref, near_ref):
    order = lax.broadcasted_iota(jnp.int32, (CH, CH), 0) >= lax.broadcasted_iota(
        jnp.int32, (CH, CH), 1
    )
    cols = cols_ref[...]
    masks = []
    for c in range(NC):
        ids_row = rows_ref[96 + 8 * c : 97 + 8 * c]
        ids_col = cols[:, 96 + 8 * c : 97 + 8 * c]
        masks.append(order & (ids_col == ids_row))
    for head in range(NH):
        at = slice(head * DH, (head + 1) * DH)
        state = None
        for c in range(NC):
            part = slice(4 * c, 4 * c + 4)
            row = 8 * c + head
            query = q_ref[part, 0, :, at].reshape(CH, DH)
            key_part = k_ref[part, 0, :, at].reshape(CH, DH)
            value_part = v_ref[part, 0, :, at].reshape(CH, DH)
            keys_across = key_part.T
            gaps = cols[:, row : row + 1] - rows_ref[row : row + 1]
            weights = jnp.where(masks[c], jnp.exp(jnp.where(masks[c], gaps, 0.0)), 0.0)
            high, low = split2(dot(query, keys_across) * weights)
            mixed = dot(high, value_part) + dot(low, value_part)
            if c:
                both = dot(query, jnp.concatenate(split2(state), axis=1))
                mixed = mixed + (both[:, :DH] + both[:, DH:]) * cols[:, 32 + row : 33 + row]
            near_ref[head, c * CH : (c + 1) * CH] = mixed
            if c < NC - 1:
                weighted = keys_across.astype(F32) * rows_ref[32 + row : 33 + row]
                both = dot(jnp.concatenate(split2(weighted), axis=0), value_part)
                own = both[:DH] + both[DH:]
                state = own if c == 0 else own + state * rows_ref[64 + row : 65 + row]


def scan_kernel(in_ref, out_ref):
    state = jnp.zeros((1, ROWS * DH), F32)
    for segment in range(out_ref.shape[0]):
        out_ref[segment] = state
        factor = jnp.concatenate([in_ref[segment, :, ROWS * DH :]] * ROWS, axis=1)
        state = state * factor + in_ref[segment, :, : ROWS * DH]


def close_kernel(place_ref, q_ref, state_ref, near_ref, cols_ref, gain_ref, out_ref):
    gain = pick_heads(gain_ref[...], place_ref[1])
    cols = cols_ref[...]
    for head in range(NH):
        at = slice(head * DH, (head + 1) * DH)
        query = q_ref[:, 0, :, at].reshape(SEG, DH)
        both = dot(query, jnp.concatenate(split2(state_ref[head]), axis=1))
        far = both[:, :DH] + both[:, DH:]
        for c in range(NC):
            column = 64 + 8 * c + head
            mixed = near_ref[head, c * CH : (c + 1) * CH] + far[c * CH : (c + 1) * CH] * (
                cols[:, column : column + 1]
            )
            square = jnp.mean(mixed * mixed, axis=-1, keepdims=True)
            normed = mixed * lax.rsqrt(square + 1e-06) * gain[head : head + 1]
            out_ref[4 * c : 4 * c + 4, :, at] = normed.astype(BF16).reshape(4, CH // 4, DH)


SMEM = pl.BlockSpec(memory_space=pltpu.SMEM)
PARAMS = pltpu.CompilerParams(vmem_limit_bytes=VMEM_LIMIT)


def part_spec(which):
    return pl.BlockSpec((GROUP, 1, SEG // GROUP, NH * DH), lambda i: (0, which, 0, 0))


def whole(*shape):
    return pl.BlockSpec(shape, lambda i: (0,) * len(shape))


def shaped(shape, kind=F32):
    return jax.ShapeDtypeStruct(shape, kind)


def local(seq_size, head_size, queries, keys, values, log_decay, doc_lengths, gain):
    tokens = queries.shape[0]
    segments = seq_size // PAIR
    pieces = NH * DH // ROWS
    seq = lax.axis_index("seq")
    place = jnp.stack([seq // PAIR, seq % PAIR]).astype(jnp.int32)
    token_groups = [
        [g * GROUP + i for i in range(GROUP)] for g in range(seq_size * head_size // GROUP)
    ]
    scan_groups = [[g * PAIR + i for g in range(segments)] for i in range(PAIR)]

    other_decay = lax.ppermute(log_decay, "seq", [(s, s ^ 1) for s in range(seq_size)])
    sent = pl.pallas_call(
        pack_kernel,
        out_shape=shaped((2, 8, 3, tokens, NH * DH), BF16),
        grid=(4,),
        in_specs=[pl.BlockSpec((tokens, 4 * NH * DH), lambda i: (0, i))] * 3,
        out_specs=pl.BlockSpec((2, 2, 3, tokens, NH * DH), lambda i: (0, i, 0, 0, 0)),
        compiler_params=PARAMS,
        name="pack",
    )(queries, keys, values).reshape(GROUP, 3, tokens, NH * DH)
    parts = lax.all_to_all(
        sent, ("seq", "head"), 0, 0, axis_index_groups=token_groups, tiled=True
    )
    own, rows, cols = pl.pallas_call(
        state_kernel,
        out_shape=(
            shaped((pieces, 1, PIECE * DH)),
            shaped((128, CH)),
            shaped((CH, 128)),
        ),
        grid=(1,),
        in_specs=[SMEM, SMEM, whole(8, SEG // PAIR), whole(8, SEG // PAIR), part_spec(1), part_spec(2)],
        out_specs=(whole(pieces, 1, PIECE * DH), whole(128, CH), whole(CH, 128)),
        compiler_params=PARAMS,
        name="state",
    )(place, doc_lengths, log_decay, other_decay, parts, parts)
    gathered = lax.all_to_all(own, "seq", 0, 0, axis_index_groups=scan_groups, tiled=True)
    near = pl.pallas_call(
        near_kernel,
        out_shape=shaped((NH, SEG, DH)),
        grid=(1,),
        in_specs=[part_spec(0), part_spec(1), part_spec(2), whole(128, CH), whole(CH, 128)],
        out_specs=whole(NH, SEG, DH),
        compiler_params=PARAMS,
        cost_estimate=pl.CostEstimate(flops=500000000, transcendentals=300000, bytes_accessed=4000000),
        name="near",
    )(parts, parts, parts, rows, cols)
    prefixes = pl.pallas_call(
        scan_kernel,
        out_shape=shaped((segments, 1, ROWS * DH)),
        name="scan",
    )(gathered)
    incoming = lax.all_to_all(
        prefixes, "seq", 0, 0, axis_index_groups=scan_groups, tiled=True
    ).reshape(NH, DH, DH)
    normed = pl.pallas_call(
        close_kernel,
        out_shape=shaped((GROUP, tokens, NH * DH), BF16),
        grid=(1,),
        in_specs=[
            SMEM,
            part_spec(0),
            whole(NH, DH, DH),
            whole(NH, SEG, DH),
            whole(CH, 128),
            whole(8, DH),
        ],
        out_specs=whole(GROUP, tokens, NH * DH),
        compiler_params=PARAMS,
        name="close",
    )(place, parts, incoming, near, cols, gain.reshape(8, DH))
    returned = lax.all_to_all(
        normed, ("seq", "head"), 0, 0, axis_index_groups=token_groups, tiled=True
    )
    return pl.pallas_call(
        unpack_kernel,
        out_shape=shaped((tokens, GROUP * NH * DH), BF16),
        grid=(4,),
        in_specs=[pl.BlockSpec((2, 2, tokens, NH * DH), lambda i: (0, i, 0, 0))],
        out_specs=pl.BlockSpec((tokens, 4 * NH * DH), lambda i: (0, i)),
        compiler_params=PARAMS,
        name="unpack",
    )(returned.reshape(2, 8, tokens, NH * DH))


def solution(mesh):
    return jax.shard_map(
        functools.partial(local, mesh.shape["seq"], mesh.shape["head"]),
        mesh=mesh,
        in_specs=(
            P(("seq", "head"), None),
            P(("seq", "head"), None),
            P(("seq", "head"), None),
            P("head", "seq"),
            P(),
            P("head"),
        ),
        out_specs=P(("seq", "head"), None),
        check_vma=False,
    )
```

```python
import functools

import jax
import jax.numpy as jnp
from jax import lax
from jax.experimental import pallas as pl
from jax.experimental.pallas import tpu as pltpu
from jax.sharding import PartitionSpec as P

F32 = jnp.float32
BF16 = jnp.bfloat16
DH = 128
CH = 128
NC = 4
PAIR = 2
NH = 4
SEG = CH * NC
GROUP = 16
XS = 4
ROWS = 16
PIECE = ROWS + 1
VMEM_LIMIT = 16 * 1024 * 1024


def split2(x):
    high = x.astype(BF16)
    return high, (x - high.astype(F32)).astype(BF16)


def split3(x):
    high = x.astype(BF16)
    rest = x - high.astype(F32)
    mid = rest.astype(BF16)
    return high, mid, (rest - mid.astype(F32)).astype(BF16)


def dot(a, b):
    return jnp.dot(a, b, preferred_element_type=F32)


def pack_kernel(k_ref, v_ref, out_ref, taken, ready, in_sems, out_sems):
    span = NH * DH
    refs = (k_ref, v_ref)
    loads, stores = [], []
    for part in range(4):
        columns = pl.ds(4 * part * span, 4 * span)
        loads.append(
            [
                pltpu.make_async_copy(
                    ref.at[:, columns], taken.at[which, :, columns], in_sems.at[part, which]
                )
                for which, ref in enumerate(refs)
            ]
        )
        stores.append(
            [
                pltpu.make_async_copy(
                    ready.at[pl.ds(8 * half + 2 * part, 2)],
                    out_ref.at[pl.ds(8 * half + 2 * part, 2)],
                    out_sems.at[part, half],
                )
                for half in range(2)
            ]
        )
    for group in loads:
        for copy in group:
            copy.start()
    for part in range(4):
        for which in range(2):
            loads[part][which].wait()
            for block in range(4):
                column = (4 * part + block) * span
                place = 8 * (block % 2) + 2 * part + block // 2
                ready[place, which] = taken[which, :, column : column + span]
        for copy in stores[part]:
            copy.start()
    for group in stores:
        for copy in group:
            copy.wait()


def fold_kernel(place_ref, q_ref, keep_ref, send_ref, sems):
    across, core = place_ref[2], place_ref[3]
    width = 2 * NH * DH
    copies = []
    for turn in range(XS):
        base = 2 * lax.rem(across + turn, XS)
        for which, ref in enumerate((keep_ref, send_ref)):
            goal = base + (core if which == 0 else 1 - core)
            columns = pl.ds(pl.multiple_of(goal * width, width), width)
            copies.append(
                pltpu.make_async_copy(q_ref.at[:, columns], ref.at[turn], sems.at[turn, which])
            )
    for copy in copies:
        copy.start()
    for copy in copies:
        copy.wait()


def weave_kernel(place_ref, keep_ref, other_ref, *slab_refs):
    core = place_ref[3]
    for turn, slab_ref in enumerate(slab_refs):
        slab_ref[core] = keep_ref[turn]
        slab_ref[1 - core] = other_ref[turn]


def regroup_kernel(place_ref, *refs):
    half, across = place_ref[1], place_ref[2]
    slab_refs, (keep_ref, send_ref) = refs[:XS], refs[XS:]
    span = NH * DH
    mine = pl.ds(pl.multiple_of(half * span, span), span)
    theirs = pl.ds(pl.multiple_of((1 - half) * span, span), span)
    for turn, slab_ref in enumerate(slab_refs):
        origin = lax.rem(across + XS - turn, XS)
        for core in range(2):
            keep_ref[2 * origin + core] = slab_ref[core, :, mine]
            send_ref[2 * origin + core] = slab_ref[core, :, theirs]


def unpack_kernel(in_ref, out_ref, ready, sems):
    tokens = in_ref.shape[1]
    span = NH * DH
    copies = []
    for row in range(tokens // 8):
        for place in range(GROUP):
            column = (2 * (place % 8) + place // 8) * span
            ready[8 * row : 8 * row + 8, column : column + span] = in_ref[
                place, 8 * row : 8 * row + 8, :
            ]
        rows = pl.ds(8 * row, 8)
        copies.append(pltpu.make_async_copy(ready.at[rows, :], out_ref.at[rows, :], sems.at[row]))
        copies[-1].start()
    for copy in copies:
        copy.wait()


def pick_heads(tile, half):
    return jnp.where(half == 0, tile, pltpu.roll(tile, 4, axis=0))


def state_kernel(place_ref, lengths_ref, own_ref, other_ref, part_ref, out_ref, rows_ref, cols_ref, send_ref, sems):
    segment, half = place_ref[0], place_ref[1]
    own, other = own_ref[...], other_ref[...]
    first = jnp.where(half == 0, own, other)
    second = jnp.where(half == 0, other, own)
    decay = jnp.concatenate(
        [
            pick_heads(part[:, i * CH : (i + 1) * CH], half)
            for part in (first, second)
            for i in range(2)
        ],
        axis=0,
    )
    upper = (
        lax.broadcasted_iota(jnp.int32, (CH, CH), 0) <= lax.broadcasted_iota(jnp.int32, (CH, CH), 1)
    ).astype(BF16)
    high, mid, low = split3(decay)
    sums = dot(high, upper) + (dot(mid, upper) + dot(low, upper))

    lane = lax.broadcasted_iota(jnp.int32, (8, CH), 1)
    start = segment * SEG
    spots = [jnp.full((8, CH), start - 1, jnp.int32)] + [start + c * CH + lane for c in range(NC)]
    ids = [jnp.zeros((8, CH), jnp.int32) for _ in spots]
    end = jnp.int32(0)
    for d in range(lengths_ref.shape[0]):
        end = end + lengths_ref[d]
        ids = [i + (end <= s).astype(jnp.int32) for i, s in zip(ids, spots)]

    def last(tile):
        return jnp.broadcast_to(tile[:, CH - 1 : CH], (8, CH))

    prior = ids[0]
    tails, leads, carries = [], [], []
    for c in range(NC):
        local, here = sums[8 * c : 8 * c + 8], ids[c + 1]
        total, closing = last(local), last(here)
        tails.append(jnp.where(here == closing, jnp.exp(total - local), 0.0))
        leads.append(jnp.where(here == prior, jnp.exp(local), 0.0))
        carries.append(jnp.where(closing == prior, jnp.exp(total), 0.0))
        prior = closing
    before = [jnp.ones((8, CH), F32)]
    for c in range(NC):
        before.append(before[-1] * carries[c])
    after = [jnp.ones((8, CH), F32)]
    for c in range(NC - 1, 0, -1):
        after.append(after[-1] * carries[c])
    after = after[::-1]
    rows_ref[0:32] = sums
    rows_ref[32:64] = jnp.concatenate(tails, axis=0)
    rows_ref[64:96] = jnp.concatenate(carries, axis=0)
    rows_ref[96:128] = jnp.concatenate([i.astype(F32) for i in ids[1:]], axis=0)
    table = jnp.concatenate(
        [sums]
        + leads
        + [lead * b for lead, b in zip(leads, before)]
        + [i.astype(F32) for i in ids[1:]],
        axis=0,
    )
    cols_ref[...] = table.T

    full_tails = [t * a for t, a in zip(tails, after)]
    copies = []
    for head in range(NH):
        at = slice(head * DH, (head + 1) * DH)
        key_part = part_ref[:, 0, :, at].reshape(SEG, DH)
        value_part = part_ref[:, 1, :, at].reshape(SEG, DH)
        weight = jnp.concatenate([t[head : head + 1] for t in full_tails], axis=1)
        weighted = key_part.T.astype(F32) * weight
        both = dot(jnp.concatenate(split2(weighted), axis=0), value_part)
        state = both[:DH] + both[DH:]
        for piece in range(DH // ROWS):
            top = (head * (DH // ROWS) + piece) * PIECE
            send_ref[top : top + ROWS] = state[piece * ROWS : (piece + 1) * ROWS]
            send_ref[top + ROWS : top + PIECE] = before[NC][head : head + 1]
        done = pl.ds(head * (DH // ROWS) * PIECE, (DH // ROWS) * PIECE)
        copies.append(pltpu.make_async_copy(send_ref.at[done], out_ref.at[done], sems.at[head]))
        copies[-1].start()
    for copy in copies:
        copy.wait()


def near_kernel(
    place_ref, own_ref, other_ref, part_ref, rows_ref, cols_ref, gain_in_ref, near_ref, scaled_ref, gain_ref
):
    half = place_ref[1]
    gain_ref[...] = pick_heads(gain_in_ref[...], half)
    order = lax.broadcasted_iota(jnp.int32, (CH, CH), 0) >= lax.broadcasted_iota(
        jnp.int32, (CH, CH), 1
    )
    cols = cols_ref[...]
    masks = []
    for c in range(NC):
        ids_row = rows_ref[96 + 8 * c : 97 + 8 * c]
        ids_col = cols[:, 96 + 8 * c : 97 + 8 * c]
        masks.append(order & (ids_col == ids_row))
    for head in range(NH):
        at = slice(head * DH, (head + 1) * DH)
        state = None
        for c in range(NC):
            part = slice(4 * c, 4 * c + 4)
            row = 8 * c + head
            blocks = slice(4 * (c % 2), 4 * (c % 2) + 4)
            query = jnp.where(
                half == c // 2, own_ref[blocks, :, at], other_ref[blocks, :, at]
            ).reshape(CH, DH)
            key_part = part_ref[part, 0, :, at].reshape(CH, DH)
            value_part = part_ref[part, 1, :, at].reshape(CH, DH)
            keys_across = key_part.T
            gaps = cols[:, row : row + 1] - rows_ref[row : row + 1]
            weights = jnp.where(masks[c], jnp.exp(jnp.where(masks[c], gaps, 0.0)), 0.0)
            high, low = split2(dot(query, keys_across) * weights)
            mixed = dot(high, value_part) + dot(low, value_part)
            if c:
                both = dot(query, jnp.concatenate(split2(state), axis=1))
                mixed = mixed + (both[:, :DH] + both[:, DH:]) * cols[:, 32 + row : 33 + row]
            near_ref[head, c * CH : (c + 1) * CH] = mixed
            high, low = split2(query.astype(F32) * cols[:, 64 + row : 65 + row])
            scaled_ref[head, c * CH : (c + 1) * CH, :DH] = high
            scaled_ref[head, c * CH : (c + 1) * CH, DH:] = low
            if c < NC - 1:
                weighted = keys_across.astype(F32) * rows_ref[32 + row : 33 + row]
                both = dot(jnp.concatenate(split2(weighted), axis=0), value_part)
                own = both[:DH] + both[DH:]
                state = own if c == 0 else own + state * rows_ref[64 + row : 65 + row]


def scan_kernel(in_ref, out_ref, ready, sems):
    segments = out_ref.shape[0]
    run = segments // 4
    state = jnp.zeros((ROWS, DH), F32)
    copies = []
    for segment in range(segments):
        ready[segment] = state
        top = segment * PIECE
        state = state * in_ref[top + ROWS : top + PIECE] + in_ref[top : top + ROWS]
        if segment % run == run - 1:
            done = pl.ds(segment + 1 - run, run)
            copies.append(
                pltpu.make_async_copy(ready.at[done], out_ref.at[done], sems.at[segment // run])
            )
            copies[-1].start()
    for copy in copies:
        copy.wait()


def close_kernel(scaled_ref, state_ref, near_ref, gain_ref, out_ref):
    averaging = jnp.full((2 * DH, DH), 1.0 / DH, BF16)
    for head in range(NH):
        high, low = split2(state_ref[head])
        right = jnp.concatenate(
            [
                jnp.concatenate([high, low], axis=1),
                jnp.concatenate([high, jnp.zeros_like(low)], axis=1),
            ],
            axis=0,
        )
        both = dot(scaled_ref[head], right)
        mixed = near_ref[head] + (both[:, :DH] + both[:, DH:])
        square = dot(jnp.concatenate(split2(mixed * mixed), axis=1), averaging)
        normed = mixed * lax.rsqrt(square + 1e-06) * gain_ref[head : head + 1]
        out_ref[:, :, head * DH : (head + 1) * DH] = normed.astype(BF16).reshape(
            GROUP, SEG // GROUP, DH
        )


SMEM = pl.BlockSpec(memory_space=pltpu.SMEM)
VMEM = pl.BlockSpec(memory_space=pltpu.VMEM)
ANY = pl.BlockSpec(memory_space=pl.ANY)
PARAMS = pltpu.CompilerParams(vmem_limit_bytes=VMEM_LIMIT)
WIDE = pltpu.CompilerParams(vmem_limit_bytes=60 * 1024 * 1024)


def shaped(shape, kind=F32):
    return jax.ShapeDtypeStruct(shape, kind)


def local(seq_size, head_size, queries, keys, values, log_decay, doc_lengths, gain):
    tokens = queries.shape[0]
    span = NH * DH
    segments = seq_size // PAIR
    pieces = NH * DH // ROWS
    seq, head = lax.axis_index("seq"), lax.axis_index("head")
    place = jnp.stack([seq // PAIR, seq % PAIR, head // 2, head % 2]).astype(jnp.int32)
    token_groups = [
        [g * GROUP + i for i in range(GROUP)] for g in range(seq_size * head_size // GROUP)
    ]
    scan_groups = [[g * PAIR + i for g in range(segments)] for i in range(PAIR)]
    pairs = [(s, s ^ 1) for s in range(seq_size)]

    other_decay = lax.ppermute(log_decay, "seq", pairs)
    sent = pl.pallas_call(
        pack_kernel,
        out_shape=shaped((GROUP, 2, tokens, span), BF16),
        in_specs=[ANY] * 2,
        out_specs=ANY,
        scratch_shapes=[
            pltpu.VMEM((2, tokens, GROUP * span), BF16),
            pltpu.VMEM((GROUP, 2, tokens, span), BF16),
            pltpu.SemaphoreType.DMA((4, 2)),
            pltpu.SemaphoreType.DMA((4, 2)),
        ],
        compiler_params=WIDE,
        name="pack",
    )(keys, values)
    parts = lax.all_to_all(
        sent, ("seq", "head"), 0, 0, axis_index_groups=token_groups, tiled=True
    )

    kept, folded = pl.pallas_call(
        fold_kernel,
        out_shape=[shaped((XS, tokens, 2 * span), BF16)] * 2,
        in_specs=[SMEM, ANY],
        out_specs=[VMEM] * 2,
        scratch_shapes=[pltpu.SemaphoreType.DMA((XS, 2))],
        compiler_params=PARAMS,
        name="fold",
    )(place, queries)
    unfolded = lax.ppermute(folded, "head", [(h, h ^ 1) for h in range(head_size)])
    slabs = pl.pallas_call(
        weave_kernel,
        out_shape=[shaped((2, tokens, 2 * span), BF16)] * XS,
        in_specs=[SMEM, VMEM, VMEM],
        out_specs=[VMEM] * XS,
        compiler_params=PARAMS,
        name="weave",
    )(place, kept, unfolded)

    own, rows, cols = pl.pallas_call(
        state_kernel,
        out_shape=(
            shaped((pieces * PIECE, DH)),
            shaped((128, CH)),
            shaped((CH, 128)),
        ),
        in_specs=[SMEM, SMEM, VMEM, VMEM, VMEM],
        out_specs=(ANY, VMEM, VMEM),
        scratch_shapes=[
            pltpu.VMEM((pieces * PIECE, DH), F32),
            pltpu.SemaphoreType.DMA((NH,)),
        ],
        compiler_params=PARAMS,
        name="state",
    )(place, doc_lengths, log_decay, other_decay, parts)
    slabs, own = lax.optimization_barrier((slabs, own))
    gathered = lax.all_to_all(
        own.reshape(pieces, 1, PIECE * DH), "seq", 0, 0, axis_index_groups=scan_groups, tiled=True
    ).reshape(pieces * PIECE, DH)
    turned = [slabs[0]] + [
        lax.ppermute(
            slabs[turn],
            "head",
            [(h, (h // 2 + turn) % XS * 2 + h % 2) for h in range(head_size)],
        )
        for turn in range(1, XS)
    ]
    kept_queries, leaving = pl.pallas_call(
        regroup_kernel,
        out_shape=[shaped((2 * XS, tokens, span), BF16)] * 2,
        in_specs=[SMEM] + [VMEM] * XS,
        out_specs=[VMEM] * 2,
        compiler_params=PARAMS,
        name="regroup",
    )(place, *turned)
    gathered, kept_queries, leaving = lax.optimization_barrier((gathered, kept_queries, leaving))
    prefixes = pl.pallas_call(
        scan_kernel,
        out_shape=shaped((segments, ROWS, DH)),
        in_specs=[VMEM],
        out_specs=ANY,
        scratch_shapes=[
            pltpu.VMEM((segments, ROWS, DH), F32),
            pltpu.SemaphoreType.DMA((4,)),
        ],
        compiler_params=PARAMS,
        name="scan",
    )(gathered)
    incoming = lax.all_to_all(
        prefixes, "seq", 0, 0, axis_index_groups=scan_groups, tiled=True
    ).reshape(NH, DH, DH)
    arriving = lax.ppermute(leaving, "seq", pairs)
    near, scaled, gains = pl.pallas_call(
        near_kernel,
        out_shape=(
            shaped((NH, SEG, DH)),
            shaped((NH, SEG, 2 * DH), BF16),
            shaped((8, DH)),
        ),
        in_specs=[SMEM] + [VMEM] * 6,
        out_specs=(VMEM, VMEM, VMEM),
        compiler_params=PARAMS,
        cost_estimate=pl.CostEstimate(flops=500000000, transcendentals=300000, bytes_accessed=4000000),
        name="near",
    )(place, kept_queries, arriving, parts, rows, cols, gain.reshape(8, DH))
    normed = pl.pallas_call(
        close_kernel,
        out_shape=shaped((GROUP, tokens, span), BF16),
        in_specs=[VMEM] * 4,
        out_specs=VMEM,
        compiler_params=PARAMS,
        name="close",
    )(scaled, incoming, near, gains)
    returned = lax.all_to_all(
        normed, ("seq", "head"), 0, 0, axis_index_groups=token_groups, tiled=True
    )
    return pl.pallas_call(
        unpack_kernel,
        out_shape=shaped((tokens, GROUP * span), BF16),
        in_specs=[VMEM],
        out_specs=ANY,
        scratch_shapes=[
            pltpu.VMEM((tokens, GROUP * span), BF16),
            pltpu.SemaphoreType.DMA((tokens // 8,)),
        ],
        compiler_params=PARAMS,
        name="unpack",
    )(returned)


def solution(mesh):
    return jax.shard_map(
        functools.partial(local, mesh.shape["seq"], mesh.shape["head"]),
        mesh=mesh,
        in_specs=(
            P(("seq", "head"), None),
            P(("seq", "head"), None),
            P(("seq", "head"), None),
            P("head", "seq"),
            P(),
            P("head"),
        ),
        out_specs=P(("seq", "head"), None),
        check_vma=False,
    )
```

```python
import functools

import jax
import jax.numpy as jnp
from jax import lax
from jax.experimental import pallas as pl
from jax.experimental.pallas import tpu as pltpu
from jax.sharding import PartitionSpec as P

F32 = jnp.float32
BF16 = jnp.bfloat16
DH = 128
CH = 128
NC = 4
PAIR = 2
NH = 4
SEG = CH * NC
XS = 4
GROUP = 16
ROWS = 16
PIECE = ROWS + 1
VMEM_LIMIT = 48 * 1024 * 1024


def split2(x):
    high = x.astype(BF16)
    return high, (x - high.astype(F32)).astype(BF16)


def split3(x):
    high = x.astype(BF16)
    rest = x - high.astype(F32)
    mid = rest.astype(BF16)
    return high, mid, (rest - mid.astype(F32)).astype(BF16)


def dot(a, b):
    return jnp.dot(a, b, preferred_element_type=F32)


def pack_kernel(k_ref, v_ref, out_ref, taken, ready, in_sems, out_sems):
    span = NH * DH
    refs = (k_ref, v_ref)
    loads, stores = [], []
    for part in range(4):
        columns = pl.ds(4 * part * span, 4 * span)
        loads.append(
            [
                pltpu.make_async_copy(
                    ref.at[:, columns], taken.at[which, :, columns], in_sems.at[part, which]
                )
                for which, ref in enumerate(refs)
            ]
        )
        stores.append(
            [
                pltpu.make_async_copy(
                    ready.at[pl.ds(8 * half + 2 * part, 2)],
                    out_ref.at[pl.ds(8 * half + 2 * part, 2)],
                    out_sems.at[part, half],
                )
                for half in range(2)
            ]
        )
    for group in loads:
        for copy in group:
            copy.start()
    for part in range(4):
        for which in range(2):
            loads[part][which].wait()
            for block in range(4):
                column = (4 * part + block) * span
                place = 8 * (block % 2) + 2 * part + block // 2
                ready[place, which] = taken[which, :, column : column + span]
        for copy in stores[part]:
            copy.start()
    for group in stores:
        for copy in group:
            copy.wait()


def unpack_kernel(in_ref, out_ref, ready, sems):
    tokens = in_ref.shape[1]
    span = NH * DH
    copies = []
    for row in range(tokens // 8):
        for place in range(GROUP):
            column = (2 * (place % 8) + place // 8) * span
            ready[8 * row : 8 * row + 8, column : column + span] = in_ref[
                place, 8 * row : 8 * row + 8, :
            ]
        rows = pl.ds(8 * row, 8)
        copies.append(pltpu.make_async_copy(ready.at[rows, :], out_ref.at[rows, :], sems.at[row]))
        copies[-1].start()
    for copy in copies:
        copy.wait()


def slab_kernel(place_ref, q_ref, *refs):
    outs, sems = refs[:XS], refs[XS]
    width = GROUP // XS * NH * DH
    copies = []
    for turn in range(XS):
        goal = lax.rem(place_ref[2] + turn, XS)
        columns = pl.ds(pl.multiple_of(goal * width, width), width)
        copies.append(pltpu.make_async_copy(q_ref.at[:, columns], outs[turn], sems.at[turn]))
    for copy in copies:
        copy.start()
    for copy in copies:
        copy.wait()


def regroup_kernel(place_ref, *refs):
    half, across, core = place_ref[1], place_ref[2], place_ref[3]
    span = NH * DH
    for far, out_ref in enumerate(refs[XS:]):
        goal = 2 * lax.rem(core + far % 2, 2) + lax.rem(half + far // 2, 2)
        columns = pl.ds(pl.multiple_of(goal * span, span), span)
        for turn, in_ref in enumerate(refs[:XS]):
            origin = lax.rem(across + XS - turn, XS)
            out_ref[origin] = in_ref[:, columns]


def settle_kernel(place_ref, *refs):
    half, core = place_ref[1], place_ref[3]
    out_ref = refs[-1]
    for far, in_ref in enumerate(refs[:-1]):
        start = 8 * lax.rem(half + far // 2, 2) + lax.rem(core + far % 2, 2)
        for origin in range(XS):
            out_ref[start + 2 * origin] = in_ref[origin]


def pick_heads(tile, half):
    return jnp.where(half == 0, tile, pltpu.roll(tile, 4, axis=0))


def state_kernel(place_ref, lengths_ref, own_ref, other_ref, part_ref, gain_in_ref, out_ref, rows_ref, cols_ref, gain_ref, send_ref, sems):
    segment, half = place_ref[0], place_ref[1]
    own, other = own_ref[...], other_ref[...]
    first = jnp.where(half == 0, own, other)
    second = jnp.where(half == 0, other, own)
    decay = jnp.concatenate(
        [
            pick_heads(part[:, i * CH : (i + 1) * CH], half)
            for part in (first, second)
            for i in range(2)
        ],
        axis=0,
    )
    upper = (
        lax.broadcasted_iota(jnp.int32, (CH, CH), 0) <= lax.broadcasted_iota(jnp.int32, (CH, CH), 1)
    ).astype(BF16)
    high, mid, low = split3(decay)
    sums = dot(high, upper) + (dot(mid, upper) + dot(low, upper))

    lane = lax.broadcasted_iota(jnp.int32, (8, CH), 1)
    start = segment * SEG
    spots = [jnp.full((8, CH), start - 1, jnp.int32)] + [start + c * CH + lane for c in range(NC)]
    ids = [jnp.zeros((8, CH), jnp.int32) for _ in spots]
    end = jnp.int32(0)
    for d in range(lengths_ref.shape[0]):
        end = end + lengths_ref[d]
        ids = [i + (end <= s).astype(jnp.int32) for i, s in zip(ids, spots)]

    def last(tile):
        return jnp.broadcast_to(tile[:, CH - 1 : CH], (8, CH))

    prior = ids[0]
    tails, leads, carries = [], [], []
    for c in range(NC):
        local, here = sums[8 * c : 8 * c + 8], ids[c + 1]
        total, closing = last(local), last(here)
        tails.append(jnp.where(here == closing, jnp.exp(total - local), 0.0))
        leads.append(jnp.where(here == prior, jnp.exp(local), 0.0))
        carries.append(jnp.where(closing == prior, jnp.exp(total), 0.0))
        prior = closing
    before = [jnp.ones((8, CH), F32)]
    for c in range(NC):
        before.append(before[-1] * carries[c])
    after = [jnp.ones((8, CH), F32)]
    for c in range(NC - 1, 0, -1):
        after.append(after[-1] * carries[c])
    after = after[::-1]
    rows_ref[0:32] = sums
    rows_ref[32:64] = jnp.concatenate(tails, axis=0)
    rows_ref[64:96] = jnp.concatenate(carries, axis=0)
    rows_ref[96:128] = jnp.concatenate([i.astype(F32) for i in ids[1:]], axis=0)
    table = jnp.concatenate(
        [sums]
        + leads
        + [lead * b for lead, b in zip(leads, before)]
        + [i.astype(F32) for i in ids[1:]],
        axis=0,
    )
    cols_ref[...] = table.T

    full_tails = [t * a for t, a in zip(tails, after)]
    gain_ref[...] = pick_heads(gain_in_ref[...], half)
    copies = []
    for head in range(NH):
        at = slice(head * DH, (head + 1) * DH)
        key_part = part_ref[:, 0, :, at].reshape(SEG, DH)
        value_part = part_ref[:, 1, :, at].reshape(SEG, DH)
        weight = jnp.concatenate([t[head : head + 1] for t in full_tails], axis=1)
        weighted = key_part.T.astype(F32) * weight
        both = dot(jnp.concatenate(split2(weighted), axis=0), value_part)
        state = both[:DH] + both[DH:]
        for piece in range(DH // ROWS):
            top = (head * (DH // ROWS) + piece) * PIECE
            send_ref[top : top + ROWS] = state[piece * ROWS : (piece + 1) * ROWS]
            send_ref[top + ROWS : top + PIECE] = before[NC][head : head + 1]
        done = pl.ds(head * (DH // ROWS) * PIECE, (DH // ROWS) * PIECE)
        copies.append(pltpu.make_async_copy(send_ref.at[done], out_ref.at[done], sems.at[head]))
        copies[-1].start()
    for copy in copies:
        copy.wait()


def near_kernel(q_ref, part_ref, rows_ref, cols_ref, near_ref, scaled_ref):
    order = lax.broadcasted_iota(jnp.int32, (CH, CH), 0) >= lax.broadcasted_iota(
        jnp.int32, (CH, CH), 1
    )
    cols = cols_ref[...]
    masks = []
    for c in range(NC):
        ids_row = rows_ref[96 + 8 * c : 97 + 8 * c]
        ids_col = cols[:, 96 + 8 * c : 97 + 8 * c]
        masks.append(order & (ids_col == ids_row))
    for head in range(NH):
        at = slice(head * DH, (head + 1) * DH)
        state = None
        for c in range(NC):
            part = slice(4 * c, 4 * c + 4)
            row = 8 * c + head
            query = q_ref[part, :, at].reshape(CH, DH)
            key_part = part_ref[part, 0, :, at].reshape(CH, DH)
            value_part = part_ref[part, 1, :, at].reshape(CH, DH)
            keys_across = key_part.T
            gaps = cols[:, row : row + 1] - rows_ref[row : row + 1]
            weights = jnp.where(masks[c], jnp.exp(jnp.where(masks[c], gaps, 0.0)), 0.0)
            high, low = split2(dot(query, keys_across) * weights)
            mixed = dot(high, value_part) + dot(low, value_part)
            if c:
                both = dot(query, jnp.concatenate(split2(state), axis=1))
                mixed = mixed + (both[:, :DH] + both[:, DH:]) * cols[:, 32 + row : 33 + row]
            near_ref[head, c * CH : (c + 1) * CH] = mixed
            high, low = split2(query.astype(F32) * cols[:, 64 + row : 65 + row])
            scaled_ref[head, c * CH : (c + 1) * CH, :DH] = high
            scaled_ref[head, c * CH : (c + 1) * CH, DH:] = low
            if c < NC - 1:
                weighted = keys_across.astype(F32) * rows_ref[32 + row : 33 + row]
                both = dot(jnp.concatenate(split2(weighted), axis=0), value_part)
                own = both[:DH] + both[DH:]
                state = own if c == 0 else own + state * rows_ref[64 + row : 65 + row]


def scan_kernel(in_ref, out_ref, ready, sems):
    segments = out_ref.shape[0]
    run = segments // 4
    state = jnp.zeros((ROWS, DH), F32)
    copies = []
    for segment in range(segments):
        ready[segment] = state
        top = segment * PIECE
        state = state * in_ref[top + ROWS : top + PIECE] + in_ref[top : top + ROWS]
        if segment % run == run - 1:
            done = pl.ds(segment + 1 - run, run)
            copies.append(
                pltpu.make_async_copy(ready.at[done], out_ref.at[done], sems.at[segment // run])
            )
            copies[-1].start()
    for copy in copies:
        copy.wait()


def close_kernel(scaled_ref, state_ref, near_ref, gain_ref, out_ref):
    averaging = jnp.full((2 * DH, DH), 1.0 / DH, BF16)
    for head in range(NH):
        high, low = split2(state_ref[head])
        right = jnp.concatenate(
            [
                jnp.concatenate([high, low], axis=1),
                jnp.concatenate([high, jnp.zeros_like(low)], axis=1),
            ],
            axis=0,
        )
        both = dot(scaled_ref[head], right)
        mixed = near_ref[head] + (both[:, :DH] + both[:, DH:])
        square = dot(jnp.concatenate(split2(mixed * mixed), axis=1), averaging)
        normed = mixed * lax.rsqrt(square + 1e-06) * gain_ref[head : head + 1]
        out_ref[:, :, head * DH : (head + 1) * DH] = normed.astype(BF16).reshape(
            GROUP, SEG // GROUP, DH
        )


SMEM = pl.BlockSpec(memory_space=pltpu.SMEM)
VMEM = pl.BlockSpec(memory_space=pltpu.VMEM)
ANY = pl.BlockSpec(memory_space=pl.ANY)
PARAMS = pltpu.CompilerParams(vmem_limit_bytes=VMEM_LIMIT)
WIDE = pltpu.CompilerParams(vmem_limit_bytes=60 * 1024 * 1024)


def shaped(shape, kind=F32):
    return jax.ShapeDtypeStruct(shape, kind)


def local(seq_size, head_size, queries, keys, values, log_decay, doc_lengths, gain):
    tokens = queries.shape[0]
    segments = seq_size // PAIR
    pieces = NH * DH // ROWS
    seq = lax.axis_index("seq")
    head = lax.axis_index("head")
    place = jnp.stack([seq // PAIR, seq % PAIR, head // 2, head % 2]).astype(jnp.int32)
    token_groups = [
        [g * GROUP + i for i in range(GROUP)] for g in range(seq_size * head_size // GROUP)
    ]
    scan_groups = [[g * PAIR + i for g in range(segments)] for i in range(PAIR)]

    other_decay = lax.ppermute(log_decay, "seq", [(s, s ^ 1) for s in range(seq_size)])
    sent = pl.pallas_call(
        pack_kernel,
        out_shape=shaped((GROUP, 2, tokens, NH * DH), BF16),
        in_specs=[ANY] * 2,
        out_specs=ANY,
        scratch_shapes=[
            pltpu.VMEM((2, tokens, GROUP * NH * DH), BF16),
            pltpu.VMEM((GROUP, 2, tokens, NH * DH), BF16),
            pltpu.SemaphoreType.DMA((4, 2)),
            pltpu.SemaphoreType.DMA((4, 2)),
        ],
        compiler_params=WIDE,
        name="pack",
    )(keys, values)
    parts = lax.all_to_all(
        sent, ("seq", "head"), 0, 0, axis_index_groups=token_groups, tiled=True
    )
    own, rows, cols, gains = pl.pallas_call(
        state_kernel,
        out_shape=(
            shaped((pieces * PIECE, DH)),
            shaped((128, CH)),
            shaped((CH, 128)),
            shaped((8, DH)),
        ),
        in_specs=[SMEM, SMEM, VMEM, VMEM, VMEM, VMEM],
        out_specs=(ANY, VMEM, VMEM, VMEM),
        scratch_shapes=[
            pltpu.VMEM((pieces * PIECE, DH), F32),
            pltpu.SemaphoreType.DMA((NH,)),
        ],
        compiler_params=PARAMS,
        name="state",
    )(place, doc_lengths, log_decay, other_decay, parts, gain.reshape(8, DH))
    span = GROUP // XS * NH * DH
    slabs = pl.pallas_call(
        slab_kernel,
        out_shape=[shaped((tokens, span), BF16)] * XS,
        in_specs=[SMEM, ANY],
        out_specs=[VMEM] * XS,
        scratch_shapes=[pltpu.SemaphoreType.DMA((XS,))],
        compiler_params=PARAMS,
        name="slab",
    )(place, queries)
    slabs, own = lax.optimization_barrier((slabs, own))
    turned = [slabs[0]] + [
        lax.ppermute(
            slabs[turn],
            "head",
            [(h, (h // 2 + turn) % XS * 2 + h % 2) for h in range(head_size)],
        )
        for turn in range(1, XS)
    ]
    grouped = pl.pallas_call(
        regroup_kernel,
        out_shape=[shaped((XS, tokens, NH * DH), BF16)] * 4,
        in_specs=[SMEM] + [VMEM] * XS,
        out_specs=[VMEM] * 4,
        compiler_params=PARAMS,
        name="regroup",
    )(place, *turned)
    gathered = lax.all_to_all(
        own.reshape(pieces, 1, PIECE * DH), "seq", 0, 0, axis_index_groups=scan_groups, tiled=True
    ).reshape(pieces * PIECE, DH)
    gathered, grouped = lax.optimization_barrier((gathered, grouped))
    prefixes = pl.pallas_call(
        scan_kernel,
        out_shape=shaped((segments, ROWS, DH)),
        in_specs=[VMEM],
        out_specs=ANY,
        scratch_shapes=[
            pltpu.VMEM((segments, ROWS, DH), F32),
            pltpu.SemaphoreType.DMA((4,)),
        ],
        compiler_params=PARAMS,
        name="scan",
    )(gathered)
    swapped = [grouped[0]] + [
        lax.ppermute(
            grouped[far],
            ("seq", "head"),
            [
                (s * head_size + h, (s ^ (far // 2)) * head_size + (h ^ (far % 2)))
                for s in range(seq_size)
                for h in range(head_size)
            ],
        )
        for far in range(1, 4)
    ]
    query_parts = pl.pallas_call(
        settle_kernel,
        out_shape=shaped((GROUP, tokens, NH * DH), BF16),
        in_specs=[SMEM] + [VMEM] * 4,
        out_specs=VMEM,
        compiler_params=PARAMS,
        name="settle",
    )(place, *swapped)
    near, scaled = pl.pallas_call(
        near_kernel,
        out_shape=(shaped((NH, SEG, DH)), shaped((NH, SEG, 2 * DH), BF16)),
        in_specs=[VMEM, VMEM, VMEM, VMEM],
        out_specs=(VMEM, VMEM),
        compiler_params=PARAMS,
        cost_estimate=pl.CostEstimate(flops=500000000, transcendentals=300000, bytes_accessed=4000000),
        name="near",
    )(query_parts, parts, rows, cols)
    incoming = lax.all_to_all(
        prefixes, "seq", 0, 0, axis_index_groups=scan_groups, tiled=True
    ).reshape(NH, DH, DH)
    normed = pl.pallas_call(
        close_kernel,
        out_shape=shaped((GROUP, tokens, NH * DH), BF16),
        in_specs=[VMEM] * 4,
        out_specs=VMEM,
        compiler_params=PARAMS,
        name="close",
    )(scaled, incoming, near, gains)
    returned = lax.all_to_all(
        normed, ("seq", "head"), 0, 0, axis_index_groups=token_groups, tiled=True
    )
    return pl.pallas_call(
        unpack_kernel,
        out_shape=shaped((tokens, GROUP * NH * DH), BF16),
        in_specs=[VMEM],
        out_specs=ANY,
        scratch_shapes=[
            pltpu.VMEM((tokens, GROUP * NH * DH), BF16),
            pltpu.SemaphoreType.DMA((tokens // 8,)),
        ],
        compiler_params=PARAMS,
        name="unpack",
    )(returned)


def solution(mesh):
    return jax.shard_map(
        functools.partial(local, mesh.shape["seq"], mesh.shape["head"]),
        mesh=mesh,
        in_specs=(
            P(("seq", "head"), None),
            P(("seq", "head"), None),
            P(("seq", "head"), None),
            P("head", "seq"),
            P(),
            P("head"),
        ),
        out_specs=P(("seq", "head"), None),
        check_vma=False,
    )
```

```python
import functools

import jax
import jax.numpy as jnp
from jax import lax
from jax.experimental import pallas as pl
from jax.experimental.pallas import tpu as pltpu
from jax.sharding import PartitionSpec as P

F32 = jnp.float32
BF16 = jnp.bfloat16
DH = 128
CH = 128
NC = 4
PAIR = 2
NH = 4
SEG = CH * NC
XS = 4
GROUP = 16
ROWS = 16
PIECE = ROWS + 1
VMEM_LIMIT = 48 * 1024 * 1024


def split2(x):
    high = x.astype(BF16)
    return high, (x - high.astype(F32)).astype(BF16)


def split3(x):
    high = x.astype(BF16)
    rest = x - high.astype(F32)
    mid = rest.astype(BF16)
    return high, mid, (rest - mid.astype(F32)).astype(BF16)


def dot(a, b):
    return jnp.dot(a, b, preferred_element_type=F32)


def pack_kernel(k_ref, v_ref, out_ref, taken, ready, in_sems, out_sems):
    span = NH * DH
    refs = (k_ref, v_ref)
    loads, stores = [], []
    for part in range(4):
        columns = pl.ds(4 * part * span, 4 * span)
        loads.append(
            [
                pltpu.make_async_copy(
                    ref.at[:, columns], taken.at[which, :, columns], in_sems.at[part, which]
                )
                for which, ref in enumerate(refs)
            ]
        )
        stores.append(
            [
                pltpu.make_async_copy(
                    ready.at[pl.ds(8 * half + 2 * part, 2)],
                    out_ref.at[pl.ds(8 * half + 2 * part, 2)],
                    out_sems.at[part, half],
                )
                for half in range(2)
            ]
        )
    for group in loads:
        for copy in group:
            copy.start()
    for part in range(4):
        for which in range(2):
            loads[part][which].wait()
            for block in range(4):
                column = (4 * part + block) * span
                place = 8 * (block % 2) + 2 * part + block // 2
                ready[place, which] = taken[which, :, column : column + span]
        for copy in stores[part]:
            copy.start()
    for group in stores:
        for copy in group:
            copy.wait()


def unpack_kernel(in_ref, out_ref, ready, sems):
    tokens = in_ref.shape[1]
    span = NH * DH
    copies = []
    for row in range(tokens // 8):
        for place in range(GROUP):
            column = (2 * (place % 8) + place // 8) * span
            ready[8 * row : 8 * row + 8, column : column + span] = in_ref[
                place, 8 * row : 8 * row + 8, :
            ]
        rows = pl.ds(8 * row, 8)
        copies.append(pltpu.make_async_copy(ready.at[rows, :], out_ref.at[rows, :], sems.at[row]))
        copies[-1].start()
    for copy in copies:
        copy.wait()


def slab_kernel(q_ref, *refs):
    outs, sems = refs[:XS], refs[XS]
    width = GROUP // XS * NH * DH
    copies = []
    for turn in range(XS):
        goal = lax.rem(whereabouts()[2] + turn, XS)
        columns = pl.ds(pl.multiple_of(goal * width, width), width)
        copies.append(pltpu.make_async_copy(q_ref.at[:, columns], outs[turn], sems.at[turn]))
    for copy in copies:
        copy.start()
    for copy in copies:
        copy.wait()


def regroup_kernel(*refs):
    half, across, core = whereabouts()[1], whereabouts()[2], whereabouts()[3]
    span = NH * DH
    for far, out_ref in enumerate(refs[XS:]):
        goal = 2 * lax.rem(core + far % 2, 2) + lax.rem(half + far // 2, 2)
        columns = pl.ds(pl.multiple_of(goal * span, span), span)
        for turn, in_ref in enumerate(refs[:XS]):
            origin = lax.rem(across + XS - turn, XS)
            out_ref[origin] = in_ref[:, columns]


def whereabouts():
    seq, head = lax.axis_index("seq"), lax.axis_index("head")
    return seq // PAIR, seq % PAIR, head // 2, head % 2


def pick_heads(tile, half):
    return jnp.where(half == 0, tile, pltpu.roll(tile, 4, axis=0))


def state_kernel(lengths_ref, own_ref, other_ref, part_ref, gain_in_ref, out_ref, rows_ref, cols_ref, gain_ref, send_ref, sems):
    segment, half = whereabouts()[0], whereabouts()[1]
    own, other = own_ref[...], other_ref[...]
    first = jnp.where(half == 0, own, other)
    second = jnp.where(half == 0, other, own)
    decay = jnp.concatenate(
        [
            pick_heads(part[:, i * CH : (i + 1) * CH], half)
            for part in (first, second)
            for i in range(2)
        ],
        axis=0,
    )
    upper = (
        lax.broadcasted_iota(jnp.int32, (CH, CH), 0) <= lax.broadcasted_iota(jnp.int32, (CH, CH), 1)
    ).astype(BF16)
    high, mid, low = split3(decay)
    sums = dot(high, upper) + (dot(mid, upper) + dot(low, upper))

    lane = lax.broadcasted_iota(jnp.int32, (8, CH), 1)
    start = segment * SEG
    spots = [jnp.full((8, CH), start - 1, jnp.int32)] + [start + c * CH + lane for c in range(NC)]
    ids = [jnp.zeros((8, CH), jnp.int32) for _ in spots]
    end = jnp.int32(0)
    for d in range(lengths_ref.shape[0]):
        end = end + lengths_ref[d]
        ids = [i + (end <= s).astype(jnp.int32) for i, s in zip(ids, spots)]

    def last(tile):
        return jnp.broadcast_to(tile[:, CH - 1 : CH], (8, CH))

    prior = ids[0]
    tails, leads, carries = [], [], []
    for c in range(NC):
        local, here = sums[8 * c : 8 * c + 8], ids[c + 1]
        total, closing = last(local), last(here)
        tails.append(jnp.where(here == closing, jnp.exp(total - local), 0.0))
        leads.append(jnp.where(here == prior, jnp.exp(local), 0.0))
        carries.append(jnp.where(closing == prior, jnp.exp(total), 0.0))
        prior = closing
    before = [jnp.ones((8, CH), F32)]
    for c in range(NC):
        before.append(before[-1] * carries[c])
    after = [jnp.ones((8, CH), F32)]
    for c in range(NC - 1, 0, -1):
        after.append(after[-1] * carries[c])
    after = after[::-1]
    floats = [i.astype(F32) for i in ids[1:]]
    for c in range(NC):
        for kind, tile in enumerate((sums[8 * c : 8 * c + 8], tails[c], carries[c], floats[c])):
            rows_ref[c, kind] = tile
    kinds = (
        [sums[8 * c : 8 * c + 8] for c in range(NC)],
        leads,
        [leads[c] * before[c] for c in range(NC)],
        floats,
    )
    table = [
        jnp.where(half == 0, tiles[first + i], tiles[2 - first + i])
        for first in (0, 2)
        for tiles in kinds
        for i in range(2)
    ]
    cols_ref[...] = jnp.concatenate(table, axis=0).T

    full_tails = [t * a for t, a in zip(tails, after)]
    gain_ref[...] = pick_heads(gain_in_ref[...], half)
    copies = []
    for head in range(NH):
        at = slice(head * DH, (head + 1) * DH)
        key_part = part_ref[:, 0, :, at].reshape(SEG, DH)
        value_part = part_ref[:, 1, :, at].reshape(SEG, DH)
        weight = jnp.concatenate([t[head : head + 1] for t in full_tails], axis=1)
        weighted = key_part.T.astype(F32) * weight
        both = dot(jnp.concatenate(split2(weighted), axis=0), value_part)
        state = both[:DH] + both[DH:]
        for piece in range(DH // ROWS):
            top = (head * (DH // ROWS) + piece) * PIECE
            send_ref[top : top + ROWS] = state[piece * ROWS : (piece + 1) * ROWS]
            send_ref[top + ROWS : top + PIECE] = before[NC][head : head + 1]
        done = pl.ds(head * (DH // ROWS) * PIECE, (DH // ROWS) * PIECE)
        copies.append(pltpu.make_async_copy(send_ref.at[done], out_ref.at[done], sems.at[head]))
        copies[-1].start()
    for copy in copies:
        copy.wait()


def chunk_state(part_ref, rows_ref, c, head, keys_across):
    at = slice(head * DH, (head + 1) * DH)
    weighted = keys_across.astype(F32) * rows_ref[c, 1, head : head + 1]
    value_part = part_ref[pl.ds(4 * c, 4), 1, :, at].reshape(CH, DH)
    both = dot(jnp.concatenate(split2(weighted), axis=0), value_part)
    return both[:DH] + both[DH:]


def keys_of(part_ref, c, head):
    at = slice(head * DH, (head + 1) * DH)
    return part_ref[pl.ds(4 * c, 4), 0, :, at].reshape(CH, DH).T


def near_half(part, shift, core, same_ref, cross_ref, part_ref, rows_ref, cols_ref, near_ref, scaled_ref):
    order = lax.broadcasted_iota(jnp.int32, (CH, CH), 0) >= lax.broadcasted_iota(
        jnp.int32, (CH, CH), 1
    )
    cols = cols_ref[:, shift : shift + 64]
    masks = [
        order & (cols[:, 48 + 8 * i : 49 + 8 * i] == rows_ref[2 * part + i, 3, 0:1])
        for i in range(2)
    ]
    for head in range(NH):
        at = slice(head * DH, (head + 1) * DH)
        first, second = (
            chunk_state(part_ref, rows_ref, c, head, keys_of(part_ref, c, head)) for c in range(2)
        )
        state = jnp.where(part == 1, second + first * rows_ref[1, 2, head : head + 1], 0.0)
        for i in range(2):
            c = 2 * part + i
            column = 8 * i + head
            same, cross = (ref[2 * i : 2 * i + 2, :, at] for ref in (same_ref, cross_ref))
            query = jnp.stack(
                [jnp.where(core == 0, same, cross), jnp.where(core == 0, cross, same)], axis=1
            ).reshape(CH, DH)
            value_part = part_ref[pl.ds(4 * c, 4), 1, :, at].reshape(CH, DH)
            keys_across = keys_of(part_ref, c, head)
            gaps = cols[:, column : column + 1] - rows_ref[c, 0, head : head + 1]
            weights = jnp.where(masks[i], jnp.exp(jnp.where(masks[i], gaps, 0.0)), 0.0)
            high, low = split2(dot(query, keys_across) * weights)
            mixed = dot(high, value_part) + dot(low, value_part)
            both = dot(query, jnp.concatenate(split2(state), axis=1))
            mixed = mixed + (both[:, :DH] + both[:, DH:]) * cols[:, 16 + column : 17 + column]
            rows = slice(i * CH, (i + 1) * CH)
            near_ref[head, rows, :] = mixed
            high, low = split2(query.astype(F32) * cols[:, 32 + column : 33 + column])
            scaled_ref[head, rows, :DH] = high
            scaled_ref[head, rows, DH:] = low
            if i == 0:
                state = chunk_state(part_ref, rows_ref, c, head, keys_across) + state * (
                    rows_ref[c, 2, head : head + 1]
                )


def near_kernel(*refs):
    near_half(whereabouts()[1], 0, whereabouts()[3], *refs)


def rest_kernel(*refs):
    near_half(1 - whereabouts()[1], 64, whereabouts()[3], *refs)


def scan_kernel(in_ref, out_ref, ready, sems):
    segments = out_ref.shape[0]
    run = segments // 4
    state = jnp.zeros((ROWS, DH), F32)
    copies = []
    for segment in range(segments):
        ready[segment] = state
        top = segment * PIECE
        state = state * in_ref[top + ROWS : top + PIECE] + in_ref[top : top + ROWS]
        if segment % run == run - 1:
            done = pl.ds(segment + 1 - run, run)
            copies.append(
                pltpu.make_async_copy(ready.at[done], out_ref.at[done], sems.at[segment // run])
            )
            copies[-1].start()
    for copy in copies:
        copy.wait()


def close_kernel(state_ref, gain_ref, own_near, own_scaled, other_near, other_scaled, out_ref):
    half = whereabouts()[1]
    averaging = jnp.full((2 * DH, DH), 1.0 / DH, BF16)
    for head in range(NH):
        high, low = split2(state_ref[head])
        right = jnp.concatenate(
            [
                jnp.concatenate([high, low], axis=1),
                jnp.concatenate([high, jnp.zeros_like(low)], axis=1),
            ],
            axis=0,
        )
        both = dot(jnp.concatenate([own_scaled[head], other_scaled[head]], axis=0), right)
        near = jnp.concatenate([own_near[head], other_near[head]], axis=0)
        mixed = near + (both[:, :DH] + both[:, DH:])
        square = dot(jnp.concatenate(split2(mixed * mixed), axis=1), averaging)
        normed = mixed * lax.rsqrt(square + 1e-06) * gain_ref[head : head + 1]
        blocks = normed.astype(BF16).reshape(GROUP, SEG // GROUP, DH)
        at = slice(head * DH, (head + 1) * DH)
        out_ref[pl.ds(8 * half, 8), :, at] = blocks[:8]
        out_ref[pl.ds(8 - 8 * half, 8), :, at] = blocks[8:]


SMEM = pl.BlockSpec(memory_space=pltpu.SMEM)
VMEM = pl.BlockSpec(memory_space=pltpu.VMEM)
ANY = pl.BlockSpec(memory_space=pl.ANY)
PARAMS = pltpu.CompilerParams(vmem_limit_bytes=VMEM_LIMIT)
WIDE = pltpu.CompilerParams(vmem_limit_bytes=60 * 1024 * 1024)


def shaped(shape, kind=F32):
    return jax.ShapeDtypeStruct(shape, kind)


def local(seq_size, head_size, queries, keys, values, log_decay, doc_lengths, gain):
    tokens = queries.shape[0]
    segments = seq_size // PAIR
    pieces = NH * DH // ROWS
    token_groups = [
        [g * GROUP + i for i in range(GROUP)] for g in range(seq_size * head_size // GROUP)
    ]
    scan_groups = [[g * PAIR + i for g in range(segments)] for i in range(PAIR)]

    other_decay = lax.ppermute(log_decay, "seq", [(s, s ^ 1) for s in range(seq_size)])
    sent = pl.pallas_call(
        pack_kernel,
        out_shape=shaped((GROUP, 2, tokens, NH * DH), BF16),
        in_specs=[ANY] * 2,
        out_specs=ANY,
        scratch_shapes=[
            pltpu.VMEM((2, tokens, GROUP * NH * DH), BF16),
            pltpu.VMEM((GROUP, 2, tokens, NH * DH), BF16),
            pltpu.SemaphoreType.DMA((4, 2)),
            pltpu.SemaphoreType.DMA((4, 2)),
        ],
        compiler_params=WIDE,
        name="pack",
    )(keys, values)
    parts = lax.all_to_all(
        sent, ("seq", "head"), 0, 0, axis_index_groups=token_groups, tiled=True
    )
    own, rows, cols, gains = pl.pallas_call(
        state_kernel,
        out_shape=(
            shaped((pieces * PIECE, DH)),
            shaped((NC, 4, 8, CH)),
            shaped((CH, 128)),
            shaped((8, DH)),
        ),
        in_specs=[SMEM, VMEM, VMEM, VMEM, VMEM],
        out_specs=(ANY, VMEM, VMEM, VMEM),
        scratch_shapes=[
            pltpu.VMEM((pieces * PIECE, DH), F32),
            pltpu.SemaphoreType.DMA((NH,)),
        ],
        compiler_params=PARAMS,
        name="state",
    )(doc_lengths, log_decay, other_decay, parts, gain.reshape(8, DH))
    span = GROUP // XS * NH * DH
    slabs = pl.pallas_call(
        slab_kernel,
        out_shape=[shaped((tokens, span), BF16)] * XS,
        in_specs=[ANY],
        out_specs=[VMEM] * XS,
        scratch_shapes=[pltpu.SemaphoreType.DMA((XS,))],
        compiler_params=PARAMS,
        name="slab",
    )(queries)
    slabs, own = lax.optimization_barrier((slabs, own))
    turned = [slabs[0]] + [
        lax.ppermute(
            slabs[turn],
            "head",
            [(h, (h // 2 + turn) % XS * 2 + h % 2) for h in range(head_size)],
        )
        for turn in range(1, XS)
    ]
    grouped = pl.pallas_call(
        regroup_kernel,
        out_shape=[shaped((XS, tokens, NH * DH), BF16)] * 4,
        in_specs=[VMEM] * XS,
        out_specs=[VMEM] * 4,
        compiler_params=PARAMS,
        name="regroup",
    )(*turned)
    gathered = lax.all_to_all(
        own.reshape(pieces, 1, PIECE * DH), "seq", 0, 0, axis_index_groups=scan_groups, tiled=True
    ).reshape(pieces * PIECE, DH)
    gathered, grouped = lax.optimization_barrier((gathered, grouped))
    prefixes = pl.pallas_call(
        scan_kernel,
        out_shape=shaped((segments, ROWS, DH)),
        in_specs=[VMEM],
        out_specs=ANY,
        scratch_shapes=[
            pltpu.VMEM((segments, ROWS, DH), F32),
            pltpu.SemaphoreType.DMA((4,)),
        ],
        compiler_params=PARAMS,
        name="scan",
    )(gathered)
    swapped = [grouped[0]] + [
        lax.ppermute(
            grouped[far],
            ("seq", "head"),
            [
                (s * head_size + h, (s ^ (far // 2)) * head_size + (h ^ (far % 2)))
                for s in range(seq_size)
                for h in range(head_size)
            ],
        )
        for far in range(1, 4)
    ]

    def near_call(kernel, name, same, cross):
        return pl.pallas_call(
            kernel,
            out_shape=(shaped((NH, SEG // 2, DH)), shaped((NH, SEG // 2, 2 * DH), BF16)),
            in_specs=[VMEM] * 5,
            out_specs=(VMEM, VMEM),
            compiler_params=PARAMS,
            cost_estimate=pl.CostEstimate(
                flops=250000000, transcendentals=150000, bytes_accessed=3000000
            ),
            name=name,
        )(same, cross, parts, rows, cols)

    near = near_call(near_kernel, "near", swapped[0], swapped[1])
    rest = near_call(rest_kernel, "rest", swapped[2], swapped[3])
    incoming = lax.all_to_all(
        prefixes, "seq", 0, 0, axis_index_groups=scan_groups, tiled=True
    ).reshape(NH, DH, DH)
    normed = pl.pallas_call(
        close_kernel,
        out_shape=shaped((GROUP, tokens, NH * DH), BF16),
        in_specs=[VMEM] * 6,
        out_specs=VMEM,
        compiler_params=PARAMS,
        name="close",
    )(incoming, gains, *near, *rest)
    returned = lax.all_to_all(
        normed, ("seq", "head"), 0, 0, axis_index_groups=token_groups, tiled=True
    )
    return pl.pallas_call(
        unpack_kernel,
        out_shape=shaped((tokens, GROUP * NH * DH), BF16),
        in_specs=[VMEM],
        out_specs=ANY,
        scratch_shapes=[
            pltpu.VMEM((tokens, GROUP * NH * DH), BF16),
            pltpu.SemaphoreType.DMA((tokens // 8,)),
        ],
        compiler_params=PARAMS,
        name="unpack",
    )(returned)


def solution(mesh):
    return jax.shard_map(
        functools.partial(local, mesh.shape["seq"], mesh.shape["head"]),
        mesh=mesh,
        in_specs=(
            P(("seq", "head"), None),
            P(("seq", "head"), None),
            P(("seq", "head"), None),
            P("head", "seq"),
            P(),
            P("head"),
        ),
        out_specs=P(("seq", "head"), None),
        check_vma=False,
    )
```

```python
import functools

import jax
import jax.numpy as jnp
from jax import lax
from jax.experimental import pallas as pl
from jax.experimental.pallas import tpu as pltpu
from jax.sharding import PartitionSpec as P

F32 = jnp.float32
BF16 = jnp.bfloat16
DH = 128
CH = 128
NC = 4
PAIR = 2
NH = 4
SEG = CH * NC
XS = 4
GROUP = 16
ROWS = 16
PIECE = ROWS + 1
VMEM_LIMIT = 48 * 1024 * 1024


def split2(x):
    high = x.astype(BF16)
    return high, (x - high.astype(F32)).astype(BF16)


def split3(x):
    high = x.astype(BF16)
    rest = x - high.astype(F32)
    mid = rest.astype(BF16)
    return high, mid, (rest - mid.astype(F32)).astype(BF16)


def dot(a, b):
    return jnp.dot(a, b, preferred_element_type=F32)


def pack_kernel(k_ref, v_ref, out_ref, taken, ready, in_sems, out_sems):
    span = NH * DH
    refs = (k_ref, v_ref)
    loads, stores = [], []
    for part in range(4):
        columns = pl.ds(4 * part * span, 4 * span)
        loads.append(
            [
                pltpu.make_async_copy(
                    ref.at[:, columns], taken.at[which, :, columns], in_sems.at[part, which]
                )
                for which, ref in enumerate(refs)
            ]
        )
        stores.append(
            [
                pltpu.make_async_copy(
                    ready.at[pl.ds(8 * half + 2 * part, 2)],
                    out_ref.at[pl.ds(8 * half + 2 * part, 2)],
                    out_sems.at[part, half],
                )
                for half in range(2)
            ]
        )
    for group in loads:
        for copy in group:
            copy.start()
    for part in range(4):
        for which in range(2):
            loads[part][which].wait()
            for block in range(4):
                column = (4 * part + block) * span
                place = 8 * (block % 2) + 2 * part + block // 2
                ready[place, which] = taken[which, :, column : column + span]
        for copy in stores[part]:
            copy.start()
    for group in stores:
        for copy in group:
            copy.wait()


def unpack_kernel(in_ref, out_ref, ready, sems):
    tokens = in_ref.shape[1]
    span = NH * DH
    copies = []
    for row in range(tokens // 8):
        for place in range(GROUP):
            column = (2 * (place % 8) + place // 8) * span
            ready[8 * row : 8 * row + 8, column : column + span] = in_ref[
                place, 8 * row : 8 * row + 8, :
            ]
        rows = pl.ds(8 * row, 8)
        copies.append(pltpu.make_async_copy(ready.at[rows, :], out_ref.at[rows, :], sems.at[row]))
        copies[-1].start()
    for copy in copies:
        copy.wait()


def slab_kernel(q_ref, *refs):
    outs, sems = refs[:XS], refs[XS]
    width = GROUP // XS * NH * DH
    copies = []
    for turn in range(XS):
        goal = lax.rem(whereabouts()[2] + turn, XS)
        columns = pl.ds(pl.multiple_of(goal * width, width), width)
        copies.append(pltpu.make_async_copy(q_ref.at[:, columns], outs[turn], sems.at[turn]))
    for copy in copies:
        copy.start()
    for copy in copies:
        copy.wait()


def regroup_kernel(*refs):
    half, across, core = whereabouts()[1], whereabouts()[2], whereabouts()[3]
    span = NH * DH
    for far, out_ref in enumerate(refs[XS:]):
        goal = 2 * lax.rem(core + far % 2, 2) + lax.rem(half + far // 2, 2)
        columns = pl.ds(pl.multiple_of(goal * span, span), span)
        for turn, in_ref in enumerate(refs[:XS]):
            origin = lax.rem(across + XS - turn, XS)
            out_ref[origin] = in_ref[:, columns]


def whereabouts():
    seq, head = lax.axis_index("seq"), lax.axis_index("head")
    return seq // PAIR, seq % PAIR, head // 2, head % 2


def pick_heads(tile, half):
    return jnp.where(half == 0, tile, pltpu.roll(tile, 4, axis=0))


def state_kernel(lengths_ref, own_ref, other_ref, part_ref, gain_in_ref, out_ref, rows_ref, cols_ref, gain_ref, send_ref, sems):
    segment, half = whereabouts()[0], whereabouts()[1]
    own, other = own_ref[...], other_ref[...]
    first = jnp.where(half == 0, own, other)
    second = jnp.where(half == 0, other, own)
    decay = jnp.concatenate(
        [
            pick_heads(part[:, i * CH : (i + 1) * CH], half)
            for part in (first, second)
            for i in range(2)
        ],
        axis=0,
    )
    upper = (
        lax.broadcasted_iota(jnp.int32, (CH, CH), 0) <= lax.broadcasted_iota(jnp.int32, (CH, CH), 1)
    ).astype(BF16)
    high, mid, low = split3(decay)
    sums = dot(high, upper) + (dot(mid, upper) + dot(low, upper))

    lane = lax.broadcasted_iota(jnp.int32, (8, CH), 1)
    start = segment * SEG
    spots = [jnp.full((8, CH), start - 1, jnp.int32)] + [start + c * CH + lane for c in range(NC)]
    ids = [jnp.zeros((8, CH), jnp.int32) for _ in spots]
    docs = lengths_ref.shape[1]
    parts = split3(jnp.broadcast_to(lengths_ref[...].astype(F32), (8, docs)))
    high, mid, low = (dot(part, upper[:docs, :docs]) for part in parts)
    ends = (high + (mid + low)).astype(jnp.int32)
    for d in range(docs):
        end = jnp.broadcast_to(ends[:, d : d + 1], (8, CH))
        ids = [i + (end <= s).astype(jnp.int32) for i, s in zip(ids, spots)]

    def last(tile):
        return jnp.broadcast_to(tile[:, CH - 1 : CH], (8, CH))

    prior = ids[0]
    tails, leads, carries = [], [], []
    for c in range(NC):
        local, here = sums[8 * c : 8 * c + 8], ids[c + 1]
        total, closing = last(local), last(here)
        tails.append(jnp.where(here == closing, jnp.exp(total - local), 0.0))
        leads.append(jnp.where(here == prior, jnp.exp(local), 0.0))
        carries.append(jnp.where(closing == prior, jnp.exp(total), 0.0))
        prior = closing
    before = [jnp.ones((8, CH), F32)]
    for c in range(NC):
        before.append(before[-1] * carries[c])
    after = [jnp.ones((8, CH), F32)]
    for c in range(NC - 1, 0, -1):
        after.append(after[-1] * carries[c])
    after = after[::-1]
    floats = [i.astype(F32) for i in ids[1:]]
    for c in range(NC):
        for kind, tile in enumerate((sums[8 * c : 8 * c + 8], tails[c], carries[c], floats[c])):
            rows_ref[c, kind] = tile
    kinds = (
        [sums[8 * c : 8 * c + 8] for c in range(NC)],
        leads,
        [leads[c] * before[c] for c in range(NC)],
        floats,
    )
    table = [
        jnp.where(half == 0, tiles[first + i], tiles[2 - first + i])
        for first in (0, 2)
        for tiles in kinds
        for i in range(2)
    ]
    cols_ref[...] = jnp.concatenate(table, axis=0).T

    full_tails = [t * a for t, a in zip(tails, after)]
    gain_ref[...] = pick_heads(gain_in_ref[...], half)
    copies = []
    for head in range(NH):
        at = slice(head * DH, (head + 1) * DH)
        key_part = part_ref[:, 0, :, at].reshape(SEG, DH)
        value_part = part_ref[:, 1, :, at].reshape(SEG, DH)
        weight = jnp.concatenate([t[head : head + 1] for t in full_tails], axis=1)
        weighted = key_part.T.astype(F32) * weight
        both = dot(jnp.concatenate(split2(weighted), axis=0), value_part)
        state = both[:DH] + both[DH:]
        for piece in range(DH // ROWS):
            top = (head * (DH // ROWS) + piece) * PIECE
            send_ref[top : top + ROWS] = state[piece * ROWS : (piece + 1) * ROWS]
            send_ref[top + ROWS : top + PIECE] = before[NC][head : head + 1]
        done = pl.ds(head * (DH // ROWS) * PIECE, (DH // ROWS) * PIECE)
        copies.append(pltpu.make_async_copy(send_ref.at[done], out_ref.at[done], sems.at[head]))
        copies[-1].start()
    for copy in copies:
        copy.wait()


def chunk_state(part_ref, rows_ref, c, head, keys_across):
    at = slice(head * DH, (head + 1) * DH)
    weighted = keys_across.astype(F32) * rows_ref[c, 1, head : head + 1]
    value_part = part_ref[pl.ds(4 * c, 4), 1, :, at].reshape(CH, DH)
    both = dot(jnp.concatenate(split2(weighted), axis=0), value_part)
    return both[:DH] + both[DH:]


def keys_of(part_ref, c, head):
    at = slice(head * DH, (head + 1) * DH)
    return part_ref[pl.ds(4 * c, 4), 0, :, at].reshape(CH, DH).T


def near_half(part, shift, core, same_ref, cross_ref, part_ref, rows_ref, cols_ref, near_ref, scaled_ref):
    order = lax.broadcasted_iota(jnp.int32, (CH, CH), 0) >= lax.broadcasted_iota(
        jnp.int32, (CH, CH), 1
    )
    cols = cols_ref[:, shift : shift + 64]
    masks = [
        order & (cols[:, 48 + 8 * i : 49 + 8 * i] == rows_ref[2 * part + i, 3, 0:1])
        for i in range(2)
    ]
    for head in range(NH):
        at = slice(head * DH, (head + 1) * DH)
        first, second = (
            chunk_state(part_ref, rows_ref, c, head, keys_of(part_ref, c, head)) for c in range(2)
        )
        state = jnp.where(part == 1, second + first * rows_ref[1, 2, head : head + 1], 0.0)
        for i in range(2):
            c = 2 * part + i
            column = 8 * i + head
            same, cross = (ref[2 * i : 2 * i + 2, :, at] for ref in (same_ref, cross_ref))
            query = jnp.stack(
                [jnp.where(core == 0, same, cross), jnp.where(core == 0, cross, same)], axis=1
            ).reshape(CH, DH)
            value_part = part_ref[pl.ds(4 * c, 4), 1, :, at].reshape(CH, DH)
            keys_across = keys_of(part_ref, c, head)
            gaps = cols[:, column : column + 1] - rows_ref[c, 0, head : head + 1]
            weights = jnp.where(masks[i], jnp.exp(jnp.where(masks[i], gaps, 0.0)), 0.0)
            high, low = split2(dot(query, keys_across) * weights)
            mixed = dot(high, value_part) + dot(low, value_part)
            both = dot(query, jnp.concatenate(split2(state), axis=1))
            mixed = mixed + (both[:, :DH] + both[:, DH:]) * cols[:, 16 + column : 17 + column]
            rows = slice(i * CH, (i + 1) * CH)
            near_ref[head, rows, :] = mixed
            high, low = split2(query.astype(F32) * cols[:, 32 + column : 33 + column])
            scaled_ref[head, rows, :DH] = high
            scaled_ref[head, rows, DH:] = low
            if i == 0:
                state = chunk_state(part_ref, rows_ref, c, head, keys_across) + state * (
                    rows_ref[c, 2, head : head + 1]
                )


def near_kernel(*refs):
    near_half(whereabouts()[1], 0, whereabouts()[3], *refs)


def rest_kernel(*refs):
    near_half(1 - whereabouts()[1], 64, whereabouts()[3], *refs)


def scan_kernel(in_ref, out_ref, ready, sems):
    segments = out_ref.shape[0]
    run = segments // 4
    state = jnp.zeros((ROWS, DH), F32)
    copies = []
    for segment in range(segments):
        ready[segment] = state
        top = segment * PIECE
        state = state * in_ref[top + ROWS : top + PIECE] + in_ref[top : top + ROWS]
        if segment % run == run - 1:
            done = pl.ds(segment + 1 - run, run)
            copies.append(
                pltpu.make_async_copy(ready.at[done], out_ref.at[done], sems.at[segment // run])
            )
            copies[-1].start()
    for copy in copies:
        copy.wait()


def close_kernel(state_ref, gain_ref, own_near, own_scaled, other_near, other_scaled, out_ref):
    half = whereabouts()[1]
    averaging = jnp.full((2 * DH, DH), 1.0 / DH, BF16)
    for head in range(NH):
        high, low = split2(state_ref[head])
        right = jnp.concatenate(
            [
                jnp.concatenate([high, low], axis=1),
                jnp.concatenate([high, jnp.zeros_like(low)], axis=1),
            ],
            axis=0,
        )
        both = dot(jnp.concatenate([own_scaled[head], other_scaled[head]], axis=0), right)
        near = jnp.concatenate([own_near[head], other_near[head]], axis=0)
        mixed = near + (both[:, :DH] + both[:, DH:])
        square = dot(jnp.concatenate(split2(mixed * mixed), axis=1), averaging)
        normed = mixed * lax.rsqrt(square + 1e-06) * gain_ref[head : head + 1]
        blocks = normed.astype(BF16).reshape(GROUP, SEG // GROUP, DH)
        at = slice(head * DH, (head + 1) * DH)
        out_ref[pl.ds(8 * half, 8), :, at] = blocks[:8]
        out_ref[pl.ds(8 - 8 * half, 8), :, at] = blocks[8:]


SMEM = pl.BlockSpec(memory_space=pltpu.SMEM)
VMEM = pl.BlockSpec(memory_space=pltpu.VMEM)
ANY = pl.BlockSpec(memory_space=pl.ANY)
PARAMS = pltpu.CompilerParams(vmem_limit_bytes=VMEM_LIMIT)
WIDE = pltpu.CompilerParams(vmem_limit_bytes=60 * 1024 * 1024)


def shaped(shape, kind=F32):
    return jax.ShapeDtypeStruct(shape, kind)


def local(seq_size, head_size, queries, keys, values, log_decay, doc_lengths, gain):
    tokens = queries.shape[0]
    segments = seq_size // PAIR
    pieces = NH * DH // ROWS
    token_groups = [
        [g * GROUP + i for i in range(GROUP)] for g in range(seq_size * head_size // GROUP)
    ]
    scan_groups = [[g * PAIR + i for g in range(segments)] for i in range(PAIR)]

    other_decay = lax.ppermute(log_decay, "seq", [(s, s ^ 1) for s in range(seq_size)])
    sent = pl.pallas_call(
        pack_kernel,
        out_shape=shaped((GROUP, 2, tokens, NH * DH), BF16),
        in_specs=[ANY] * 2,
        out_specs=ANY,
        scratch_shapes=[
            pltpu.VMEM((2, tokens, GROUP * NH * DH), BF16),
            pltpu.VMEM((GROUP, 2, tokens, NH * DH), BF16),
            pltpu.SemaphoreType.DMA((4, 2)),
            pltpu.SemaphoreType.DMA((4, 2)),
        ],
        compiler_params=WIDE,
        name="pack",
    )(keys, values)
    parts = lax.all_to_all(
        sent, ("seq", "head"), 0, 0, axis_index_groups=token_groups, tiled=True
    )
    own, rows, cols, gains = pl.pallas_call(
        state_kernel,
        out_shape=(
            shaped((pieces * PIECE, DH)),
            shaped((NC, 4, 8, CH)),
            shaped((CH, 128)),
            shaped((8, DH)),
        ),
        in_specs=[VMEM, VMEM, VMEM, VMEM, VMEM],
        out_specs=(ANY, VMEM, VMEM, VMEM),
        scratch_shapes=[
            pltpu.VMEM((pieces * PIECE, DH), F32),
            pltpu.SemaphoreType.DMA((NH,)),
        ],
        compiler_params=PARAMS,
        name="state",
    )(doc_lengths.reshape(1, -1), log_decay, other_decay, parts, gain.reshape(8, DH))
    span = GROUP // XS * NH * DH
    slabs = pl.pallas_call(
        slab_kernel,
        out_shape=[shaped((tokens, span), BF16)] * XS,
        in_specs=[ANY],
        out_specs=[VMEM] * XS,
        scratch_shapes=[pltpu.SemaphoreType.DMA((XS,))],
        compiler_params=PARAMS,
        name="slab",
    )(queries)
    slabs, own = lax.optimization_barrier((slabs, own))
    turned = [slabs[0]] + [
        lax.ppermute(
            slabs[turn],
            "head",
            [(h, (h // 2 + turn) % XS * 2 + h % 2) for h in range(head_size)],
        )
        for turn in range(1, XS)
    ]
    grouped = pl.pallas_call(
        regroup_kernel,
        out_shape=[shaped((XS, tokens, NH * DH), BF16)] * 4,
        in_specs=[VMEM] * XS,
        out_specs=[VMEM] * 4,
        compiler_params=PARAMS,
        name="regroup",
    )(*turned)
    gathered = lax.all_to_all(
        own.reshape(pieces, 1, PIECE * DH), "seq", 0, 0, axis_index_groups=scan_groups, tiled=True
    ).reshape(pieces * PIECE, DH)
    gathered, grouped = lax.optimization_barrier((gathered, grouped))
    prefixes = pl.pallas_call(
        scan_kernel,
        out_shape=shaped((segments, ROWS, DH)),
        in_specs=[VMEM],
        out_specs=ANY,
        scratch_shapes=[
            pltpu.VMEM((segments, ROWS, DH), F32),
            pltpu.SemaphoreType.DMA((4,)),
        ],
        compiler_params=PARAMS,
        name="scan",
    )(gathered)
    swapped = [grouped[0]] + [
        lax.ppermute(
            grouped[far],
            ("seq", "head"),
            [
                (s * head_size + h, (s ^ (far // 2)) * head_size + (h ^ (far % 2)))
                for s in range(seq_size)
                for h in range(head_size)
            ],
        )
        for far in range(1, 4)
    ]

    def near_call(kernel, name, same, cross):
        return pl.pallas_call(
            kernel,
            out_shape=(shaped((NH, SEG // 2, DH)), shaped((NH, SEG // 2, 2 * DH), BF16)),
            in_specs=[VMEM] * 5,
            out_specs=(VMEM, VMEM),
            compiler_params=PARAMS,
            cost_estimate=pl.CostEstimate(
                flops=250000000, transcendentals=150000, bytes_accessed=3000000
            ),
            name=name,
        )(same, cross, parts, rows, cols)

    near = near_call(near_kernel, "near", swapped[0], swapped[1])
    rest = near_call(rest_kernel, "rest", swapped[2], swapped[3])
    incoming = lax.all_to_all(
        prefixes, "seq", 0, 0, axis_index_groups=scan_groups, tiled=True
    ).reshape(NH, DH, DH)
    normed = pl.pallas_call(
        close_kernel,
        out_shape=shaped((GROUP, tokens, NH * DH), BF16),
        in_specs=[VMEM] * 6,
        out_specs=VMEM,
        compiler_params=PARAMS,
        name="close",
    )(incoming, gains, *near, *rest)
    returned = lax.all_to_all(
        normed, ("seq", "head"), 0, 0, axis_index_groups=token_groups, tiled=True
    )
    return pl.pallas_call(
        unpack_kernel,
        out_shape=shaped((tokens, GROUP * NH * DH), BF16),
        in_specs=[VMEM],
        out_specs=ANY,
        scratch_shapes=[
            pltpu.VMEM((tokens, GROUP * NH * DH), BF16),
            pltpu.SemaphoreType.DMA((tokens // 8,)),
        ],
        compiler_params=PARAMS,
        name="unpack",
    )(returned)


def solution(mesh):
    return jax.shard_map(
        functools.partial(local, mesh.shape["seq"], mesh.shape["head"]),
        mesh=mesh,
        in_specs=(
            P(("seq", "head"), None),
            P(("seq", "head"), None),
            P(("seq", "head"), None),
            P("head", "seq"),
            P(),
            P("head"),
        ),
        out_specs=P(("seq", "head"), None),
        check_vma=False,
    )
```
